256 devices in a mesh: row: 8 (over z_hi, x), col: 32 (over z_lo, y, core).
Axes of the slice: x: 4, y: 4, z: 8 (z_hi: 2, z_lo: 4; z = z_hi * 4 + z_lo), core: 2. Of those that a mesh axis runs over, the one named last changes fastest.
Arguments:
- contexts: bfloat16 [32768, 128], P(('row', 'col')), may hold values from -8 to 8
- logged_actions: int32 [32768], P(('row', 'col')), may hold values from 0 to 131041
- policy_actions: int32 [32768, 8], P(('row', 'col')), may hold values from 0 to 131041
- rewards: float32 [32768], P(('row', 'col')), may hold values from 0.2 to 2
Outputs:
- weights: float32 [32768, 8], P(('row', 'col'))
- residual: float32 [32768, 8], P(('row', 'col'))
- values: float32 [8], replicated
The draws below stay inside these ranges and needn't reach their ends.
All inputs are finite; a program needn't handle non-finite values.
Results may differ from the reference program's by a relative error of at most 0.0056.
Values may be sent and summed in bfloat16 or wider, within the bound.
No kernel may reach another device: no remote copies, remote signals or barrier semaphores. Data moves between devices by JAX's collectives and lax.ppermute only.
A program may use at most 64 MiB of HBM per device.

```python
import math
import jax
import jax.numpy as jnp
from jax import lax

D = 128
NPOL = 8
NACT = 16
CATALOG = 131042
TOTAL = 32768


latent_dims = 8


def draw_contexts(key, part):
    latent_key, jitter_key, coef_key, rough_key = jax.random.split(key, 4)
    latent = jnp.clip(jax.random.normal(latent_key, (TOTAL, latent_dims), jnp.float32), -3.0, 3.0)
    fine_jitter = jnp.clip(jax.random.normal(jitter_key, (TOTAL, D), jnp.float32), -4.0, 4.0)
    coefficients = jax.random.uniform(coef_key, (D,), jnp.float32, 1.0, 1.7)
    feature_latent = jnp.arange(D, dtype=jnp.int32) % latent_dims
    spread = latent[:, feature_latent] * coefficients[None, :] + 0.3 * fine_jitter
    ramp_scale = 0.6 + 0.6 * jnp.arange(TOTAL, dtype=jnp.float32) / TOTAL
    roughness = jnp.exp(jax.random.uniform(rough_key, (TOTAL,), jnp.float32, -0.1, 0.1))
    placed = spread * (ramp_scale * roughness)[:, None]
    return jnp.clip(placed, -7.9, 7.9).astype(jnp.bfloat16)


def draw_logged_actions(key, part):
    own_key = jax.random.fold_in(key, 11)
    drawn = jax.random.randint(own_key, (TOTAL,), 0, CATALOG, dtype=jnp.int32)
    return drawn.at[0].set(0).at[TOTAL - 1].set(CATALOG - 1).astype(jnp.int32)


def draw_policy_actions(key, part):
    own_key = jax.random.fold_in(key, 23)
    drawn = jax.random.randint(own_key, (TOTAL, NPOL), 0, CATALOG, dtype=jnp.int32)
    return drawn.at[0, 0].set(0).at[TOTAL - 1, NPOL - 1].set(CATALOG - 1).astype(jnp.int32)


def shard_levels(rng, shape, pieces, least, largest):
    factor_of, own = 1.0, jax.random.fold_in(rng, 6)
    for axis_at, shards_of in pieces:
        heights = jnp.exp(jax.random.uniform(jax.random.fold_in(own, axis_at), (shards_of,), jnp.float32, least / len(pieces), largest / len(pieces)))
        factor_of = factor_of * jnp.repeat(heights, shape[axis_at] // shards_of).reshape([-1 if axis == axis_at else 1 for axis in range(len(shape))])
    return factor_of


def setup_inputs(seed: int = 0) -> dict:
    key_list = jax.random.split(jax.random.key(seed), 5)
    contexts = draw_contexts(jax.random.fold_in(key_list[4], 71), 0)
    logged_actions = draw_logged_actions(jax.random.fold_in(key_list[4], 71), 0)
    policy_actions = draw_policy_actions(jax.random.fold_in(key_list[4], 71), 0)
    rewards = jnp.clip(jnp.exp(math.log(2.0) - 2.3025851 * jax.random.uniform(key_list[3], (TOTAL,), jnp.float32) ** shard_levels(key_list[3], (TOTAL,), ((0, 256),), -0.2, 0.2)), 0.2, 2.0)
    return dict(contexts=contexts, logged_actions=logged_actions, policy_actions=policy_actions, rewards=rewards)


ridge = 0.1
stride_base = 1009
phase_step = 0.37
two_pi = 2.0 * math.pi

def action_features(chosen, width):
    levels = jnp.arange(width, dtype=jnp.int32)
    multipliers = 1 + stride_base * levels
    turned = chosen[..., None].astype(jnp.int32) * multipliers % CATALOG
    angles = turned.astype(jnp.float32) * (two_pi / CATALOG) + phase_step * levels.astype(jnp.float32)
    wave_terms = math.sqrt(2.0 / width) * jnp.cos(angles)
    constant_term = jnp.full(wave_terms.shape, 1.0 / math.sqrt(width), jnp.float32)
    return jnp.where(levels == 0, constant_term, wave_terms).astype(jnp.bfloat16)

def select_actions(products, onehot):
    shaped = products.reshape(products.shape[:-1] + (products.shape[-1] // onehot.shape[-1], onehot.shape[-1]))
    return lax.optimization_barrier(jnp.sum(shaped * jnp.expand_dims(onehot.astype(jnp.float32), -2), axis=-1))

def kernel_rows(block, everything, block_sq, all_squares):
    inner = jnp.dot(block, everything.T, preferred_element_type=jnp.float32)
    return jnp.exp((2.0 * inner - block_sq[:, None] - all_squares[None, :]) / everything.shape[1]).astype(jnp.bfloat16)

def reference(contexts, logged_actions, policy_actions, rewards):
    factor = NACT / TOTAL
    squares = lax.optimization_barrier(jnp.sum(contexts.astype(jnp.float32) ** 2, axis=1))
    logged_onehot = action_features(logged_actions, NACT)
    policy_onehot = action_features(policy_actions, NACT).reshape(TOTAL, NPOL * NACT)
    step_rows = 512
    blocks = TOTAL // step_rows
    context_blocks = contexts.reshape(blocks, step_rows, D)
    square_blocks = squares.reshape(blocks, step_rows)
    onehot_blocks = logged_onehot.reshape(blocks, step_rows, NACT)

    def first_sweep(block_args):
        block, block_sq, block_onehot = block_args
        kernel = kernel_rows(block, contexts, block_sq, squares)
        return factor * select_actions(jnp.dot(kernel, policy_onehot, preferred_element_type=jnp.float32), block_onehot)
    right_side = lax.map(first_sweep, (context_blocks, square_blocks, onehot_blocks)).reshape(TOTAL, NPOL)
    right_low = right_side.astype(jnp.bfloat16)
    matched = (logged_onehot[:, None, :] * right_low[:, :, None]).astype(jnp.bfloat16).reshape(TOTAL, NPOL * NACT)
    right_blocks = right_side.reshape(blocks, step_rows, NPOL)

    def second_sweep(block_args):
        block, block_sq, block_onehot, block_right = block_args
        kernel = kernel_rows(block, contexts, block_sq, squares)
        applied = select_actions(jnp.dot(kernel, matched, preferred_element_type=jnp.float32), block_onehot)
        return factor * applied + ridge * block_right
    image = lax.map(second_sweep, (context_blocks, square_blocks, onehot_blocks, right_blocks)).reshape(TOTAL, NPOL)
    norm_sums = lax.optimization_barrier(jnp.sum(right_side * right_side, axis=0))
    curvature = lax.optimization_barrier(jnp.sum(right_side * image, axis=0))
    reward_sums = lax.optimization_barrier(jnp.sum(rewards[:, None] * right_side, axis=0))
    alpha = norm_sums / curvature
    weights = alpha[None, :] * right_side
    residual = right_side - alpha[None, :] * image
    values = alpha * reward_sums / TOTAL
    return (weights, residual, values)
```

```python
import math

import jax
import jax.numpy as jnp
from jax import lax
from jax.experimental import pallas as pl
from jax.experimental.pallas import tpu as pltpu
from jax.sharding import Mesh
from jax.sharding import PartitionSpec as P

NPOL = 8
NACT = 16
CATALOG = 131042
D = 128
TILE = 128

ridge = 0.1
stride_base = 1009
phase_step = 0.37
two_pi = 2.0 * math.pi

SIZES = (("z_hi", 2), ("x", 4), ("z_lo", 4), ("y", 4), ("core", 2))
EVERY = tuple(name for name, _ in SIZES)
PLANE = ("x", "y")
COLUMN = ("z_hi", "z_lo")
PLANES = 16
COLUMNS = 8
LEFT = 2 * PLANES
ROWS = 176
FEAT_AT, CODE_AT = 128, 144
RIGHT_ROWS = 144

f32, bf16, i32 = jnp.float32, jnp.bfloat16, jnp.int32
MIB = 1 << 20


def wrap(product):
    guess = (product.astype(f32) * (1.0 / CATALOG)).astype(i32)
    left = product - guess * CATALOG
    left = jnp.where(left < 0, left + CATALOG, left)
    return jnp.where(left >= CATALOG, left - CATALOG, left)


def cos_sin(turn):
    eighth = (turn.astype(f32) * (4.0 / CATALOG) + 0.5).astype(i32)
    rest = 4 * turn - eighth * CATALOG
    t = rest.astype(f32) * (two_pi / 4 / CATALOG)
    u = t * t
    s = t * (1.0 + u * (-1.0 / 6 + u * (1.0 / 120 + u * (-1.0 / 5040 + u * (1.0 / 362880)))))
    c = 1.0 + u * (-0.5 + u * (1.0 / 24 + u * (-1.0 / 720 + u * (1.0 / 40320))))
    swap = (eighth == 1) | (eighth == 3)
    a = jnp.where(swap, s, c)
    b = jnp.where(swap, c, s)
    a = jnp.where((eighth == 1) | (eighth == 2), -a, a)
    b = jnp.where((eighth == 2) | (eighth == 3), -b, b)
    return a, b


def features(chosen):
    amp = math.sqrt(2.0 / NACT)
    c0, s0 = cos_sin(chosen)
    cz, sz = cos_sin(wrap(chosen * stride_base))
    pc, ps = math.cos(phase_step), math.sin(phase_step)
    zr = cz * pc - sz * ps
    zi = cz * ps + sz * pc
    wr, wi = c0 * amp, s0 * amp
    out = [jnp.full(chosen.shape, 1.0 / math.sqrt(NACT), f32)]
    for _ in range(1, NACT):
        wr, wi = wr * zr - wi * zi, wr * zi + wi * zr
        out.append(wr)
    return out


def prepare(ctx_ref, logged_ref, policy_ref, plane_ref, column_ref):
    feats = features(logged_ref[...])
    logged = jnp.concatenate(feats, axis=0)
    acts = policy_ref[...]
    high = acts >> 16
    middle = (acts >> 8) & 255
    low = acts & 255
    codes = jnp.concatenate([high, middle, low, jnp.zeros_like(low)], axis=0).astype(f32)
    small = jnp.concatenate([logged, codes], axis=0).astype(bf16)
    ctx = ctx_ref[...]
    for i in range(PLANES):
        plane_ref[i, :TILE, :] = ctx
        plane_ref[i, TILE:, :] = small
    for i in range(COLUMNS):
        column_ref[i, :TILE, :] = ctx
        column_ref[i, TILE:, :] = small[:NACT]


SCALE = math.log2(math.e) / D


def first_kernel(own_ref, other_ref, right_ref, kernel_ref, sums_ref, policy, squares, acc):
    step = pl.program_id(0)

    @pl.when(step == 0)
    def _():
        for half, ref in enumerate((own_ref, other_ref)):
            def decode(j, carry):
                codes = ref[j, CODE_AT : CODE_AT + 32, :].astype(f32).astype(i32)
                acts = (codes[0:8] << 16) + (codes[8:16] << 8) + codes[16:24]
                feats = jnp.concatenate(features(acts), axis=0).astype(bf16)
                policy[j, :, half * TILE : (half + 1) * TILE] = feats
                return carry
            lax.fori_loop(0, PLANES, decode, 0, unroll=4)
        for b in range(COLUMNS):
            x = right_ref[b, :TILE, :].astype(f32)
            total = jnp.sum(x * x, axis=1, keepdims=True) * SCALE
            squares[:, b * TILE : (b + 1) * TILE] = jnp.transpose(jnp.broadcast_to(total, (TILE, TILE)))[:8]
        acc[...] = jnp.zeros_like(acc)

    for half, ref in enumerate((own_ref, other_ref)):
        rows = ref[step, :TILE, :]
        wide = rows.astype(f32)
        row_sq = jnp.sum(wide * wide, axis=1, keepdims=True) * SCALE
        for b in range(0, COLUMNS, 2):
            cols = right_ref[b : b + 2, :TILE, :].reshape(2 * TILE, D)
            inner = lax.dot_general(rows, cols, (((1,), (1,)), ((), ())), preferred_element_type=f32)
            span = slice(b * TILE, (b + 2) * TILE)
            expo = (2.0 * SCALE) * inner - row_sq - squares[0:1, span]
            kernel_ref[half * TILE : (half + 1) * TILE, span] = jnp.exp2(expo).astype(bf16)
    acc[...] += jnp.dot(policy[step], kernel_ref[...], preferred_element_type=f32)

    @pl.when(step == pl.num_programs(0) - 1)
    def _():
        for b in range(COLUMNS):
            chosen = right_ref[b, FEAT_AT : FEAT_AT + NACT, :].astype(f32)
            total = jnp.zeros((NPOL, TILE), f32)
            for c in range(NACT):
                total += acc[c * NPOL : (c + 1) * NPOL, b * TILE : (b + 1) * TILE] * chosen[c : c + 1]
            for peer in range(COLUMNS):
                sums_ref[peer, b] = total


def second_kernel(place_ref, kernel_ref, parts_ref, right_ref, own_ref, other_ref, image_ref, side_ref, matched):
    step = pl.program_id(0)
    factor = NACT / (TILE * LEFT * COLUMNS)

    @pl.when(step == 0)
    def _():
        for b in range(COLUMNS):
            total = parts_ref[0, b]
            for peer in range(1, COLUMNS):
                total += parts_ref[peer, b]
            total = total * factor
            side_ref[b] = total
            low = total.astype(bf16).astype(f32)
            chosen = right_ref[b, FEAT_AT : FEAT_AT + NACT, :].astype(f32)
            made = jnp.concatenate([chosen[c : c + 1] * low for c in range(NACT)], axis=0)
            matched[:, b * TILE : (b + 1) * TILE] = made.astype(bf16)

    out = lax.dot_general(matched[...], kernel_ref[...], (((1,), (1,)), ((), ())), preferred_element_type=f32)
    core = place_ref[0]
    for half, ref in enumerate((own_ref, other_ref)):
        chosen = ref[step, FEAT_AT : FEAT_AT + NACT, :].astype(f32)
        total = jnp.zeros((NPOL, TILE), f32)
        for c in range(NACT):
            total += out[c * NPOL : (c + 1) * NPOL, half * TILE : (half + 1) * TILE] * chosen[c : c + 1]
        image_ref[0, jnp.where(core == half, 0, 1)] = total * factor


def third_kernel(place_ref, parts_ref, side_ref, rewards_ref, image_ref, own_ref, sums_ref):
    total = parts_ref[0]
    for i in range(1, LEFT):
        total += parts_ref[i]
    side = side_ref[place_ref[1]]
    image = total + ridge * side
    image_ref[...] = image
    own_ref[...] = side
    lane = lax.broadcasted_iota(i32, (NPOL, TILE), 1)
    row = lax.broadcasted_iota(i32, (NPOL, TILE), 0)
    spread = jnp.zeros((NPOL, TILE), f32)
    for k, value in enumerate((side * side, side * image, rewards_ref[...] * side)):
        spread = jnp.where(lane == row + k * NPOL, jnp.sum(value, axis=1, keepdims=True), spread)
    flat = jnp.sum(spread, axis=0, keepdims=True)
    sums_ref[...] = jnp.broadcast_to(flat, sums_ref.shape)


def last_kernel(sums_ref, image_ref, side_ref, weights_ref, residual_ref, values_ref):
    count = sums_ref.shape[0]
    total = jnp.sum(sums_ref[...], axis=0, keepdims=True)
    lane = lax.broadcasted_iota(i32, (NPOL, TILE), 1)
    row = lax.broadcasted_iota(i32, (NPOL, TILE), 0)
    wide = jnp.broadcast_to(total, (NPOL, TILE))

    def pick(k):
        return jnp.sum(jnp.where(lane == row + k * NPOL, wide, 0.0), axis=1, keepdims=True)

    alpha = pick(0) / pick(1)
    side = side_ref[...]
    weights_ref[...] = alpha * side
    residual_ref[...] = side - alpha * image_ref[...]
    values = alpha * pick(2) / (TILE * count)
    values_ref[...] = jnp.sum(jnp.where(lane == row, values, 0.0), axis=0, keepdims=True)


def params(limit=48 * MIB, grid=False):
    return pltpu.CompilerParams(
        vmem_limit_bytes=limit, dimension_semantics=("arbitrary",) if grid else None
    )


def exchange(value, axes):
    return lax.all_to_all(value, axes, 0, 0)


def on_device(contexts, logged_actions, policy_actions, rewards):
    core = lax.axis_index("core")
    column = lax.axis_index(COLUMN)
    place = jnp.stack([core, column]).astype(i32)
    sds = jax.ShapeDtypeStruct

    plane_send, column_send = pl.pallas_call(
        prepare,
        out_shape=(sds((PLANES, ROWS, D), bf16), sds((COLUMNS, RIGHT_ROWS, D), bf16)),
        compiler_params=params(),
    )(contexts, logged_actions.reshape(1, TILE), policy_actions.T)
    own = exchange(plane_send, PLANE)
    other = lax.ppermute(own, "core", [(0, 1), (1, 0)])
    right = exchange(column_send, COLUMN)

    whole = lambda shape: pl.BlockSpec(shape, lambda i, *_: (0,) * len(shape), pipeline_mode=pl.Buffered(1))
    left_spec, right_spec = whole((PLANES, ROWS, D)), whole((COLUMNS, RIGHT_ROWS, D))
    part_shape = (COLUMNS, COLUMNS, NPOL, TILE)
    width = COLUMNS * TILE
    kernel_spec = pl.BlockSpec((2 * TILE, width), lambda i, *_: (i, 0))
    kernel, first = pl.pallas_call(
        first_kernel,
        grid=(PLANES,),
        in_specs=[left_spec, left_spec, right_spec],
        out_specs=(kernel_spec, pl.BlockSpec(part_shape, lambda i: (0, 0, 0, 0))),
        out_shape=(sds((LEFT * TILE, width), bf16), sds(part_shape, f32)),
        scratch_shapes=[
            pltpu.VMEM((PLANES, TILE, 2 * TILE), bf16),
            pltpu.VMEM((8, width), f32),
            pltpu.VMEM((TILE, width), f32),
        ],
        compiler_params=params(grid=True),
    )(own, other, right)
    parts = exchange(first, COLUMN)

    image_parts, side = pl.pallas_call(
        second_kernel,
        grid_spec=pltpu.PrefetchScalarGridSpec(
            num_scalar_prefetch=1,
            grid=(PLANES,),
            in_specs=[kernel_spec, whole(part_shape), right_spec, left_spec, left_spec],
            out_specs=(
                pl.BlockSpec((1, 2, NPOL, TILE), lambda i, *_: (i, 0, 0, 0)),
                pl.BlockSpec((COLUMNS, NPOL, TILE), lambda i, *_: (0, 0, 0)),
            ),
            scratch_shapes=[pltpu.VMEM((TILE, width), bf16)],
        ),
        out_shape=(sds((PLANES, 2, NPOL, TILE), f32), sds((COLUMNS, NPOL, TILE), f32)),
        compiler_params=params(grid=True),
    )(place, kernel, parts, right, own, other)
    image_parts = exchange(image_parts.reshape(LEFT, NPOL, TILE), PLANE + ("core",))

    count = LEFT * COLUMNS
    vmem = pl.BlockSpec(memory_space=pltpu.VMEM)
    image, own_side, sums = pl.pallas_call(
        third_kernel,
        in_specs=[pl.BlockSpec(memory_space=pltpu.SMEM), vmem, vmem, vmem],
        out_shape=(sds((NPOL, TILE), f32), sds((NPOL, TILE), f32), sds((count, TILE), f32)),
        compiler_params=params(),
    )(place, image_parts, side, rewards.reshape(1, TILE))
    sums = exchange(sums.reshape(count, 1, TILE), EVERY).reshape(count, TILE)
    weights, residual, values = pl.pallas_call(
        last_kernel,
        out_shape=(sds((NPOL, TILE), f32), sds((NPOL, TILE), f32), sds((1, TILE), f32)),
        compiler_params=params(),
    )(sums, image, own_side)
    return weights.T, residual.T, values[0, :NPOL]


def solution(mesh):
    fine = Mesh(mesh.devices.reshape([size for _, size in SIZES]), EVERY)
    return jax.shard_map(
        on_device,
        mesh=fine,
        in_specs=(P(EVERY, None), P(EVERY), P(EVERY, None), P(EVERY)),
        out_specs=(P(EVERY, None), P(EVERY, None), P()),
        check_vma=False,
    )
```

```python
import math

import jax
import jax.numpy as jnp
from jax import lax
from jax.experimental import pallas as pl
from jax.experimental.pallas import tpu as pltpu
from jax.sharding import Mesh
from jax.sharding import PartitionSpec as P

NPOL = 8
NACT = 16
CATALOG = 131042
D = 128
TILE = 128

ridge = 0.1
stride_base = 1009
phase_step = 0.37
two_pi = 2.0 * math.pi

SIZES = (("z_hi", 2), ("x", 4), ("z_lo", 4), ("y", 4), ("core", 2))
EVERY = tuple(name for name, _ in SIZES)
PLANE = ("x", "y")
COLUMN = ("z_hi", "z_lo")
PLANES = 16
COLUMNS = 8
LEFT = 2 * PLANES
ROWS = 160
FEAT_AT, CODE_AT = 128, 144
RIGHT_ROWS = 144

f32, bf16, i32 = jnp.float32, jnp.bfloat16, jnp.int32
MIB = 1 << 20


def wrap(product):
    guess = (product.astype(f32) * (1.0 / CATALOG)).astype(i32)
    left = product - guess * CATALOG
    left = jnp.where(left < 0, left + CATALOG, left)
    return jnp.where(left >= CATALOG, left - CATALOG, left)


def cos_sin(turn):
    eighth = (turn.astype(f32) * (4.0 / CATALOG) + 0.5).astype(i32)
    rest = 4 * turn - eighth * CATALOG
    t = rest.astype(f32) * (two_pi / 4 / CATALOG)
    u = t * t
    s = t * (1.0 + u * (-1.0 / 6 + u * (1.0 / 120 + u * (-1.0 / 5040 + u * (1.0 / 362880)))))
    c = 1.0 + u * (-0.5 + u * (1.0 / 24 + u * (-1.0 / 720 + u * (1.0 / 40320))))
    swap = (eighth == 1) | (eighth == 3)
    a = jnp.where(swap, s, c)
    b = jnp.where(swap, c, s)
    a = jnp.where((eighth == 1) | (eighth == 2), -a, a)
    b = jnp.where((eighth == 2) | (eighth == 3), -b, b)
    return a, b


def features(chosen):
    amp = math.sqrt(2.0 / NACT)
    c0, s0 = cos_sin(chosen)
    cz, sz = cos_sin(wrap(chosen * stride_base))
    pc, ps = math.cos(phase_step), math.sin(phase_step)
    zr = cz * pc - sz * ps
    zi = cz * ps + sz * pc
    wr, wi = c0 * amp, s0 * amp
    out = [jnp.full(chosen.shape, 1.0 / math.sqrt(NACT), f32)]
    for _ in range(1, NACT):
        wr, wi = wr * zr - wi * zi, wr * zi + wi * zr
        out.append(wr)
    return out


def prepare(ctx_hbm, logged_hbm, policy_hbm, plane_ref, column_ref, ctx_ref, logged_ref, policy_ref, sems):
    moves = [
        pltpu.make_async_copy(source, target, sems.at[i])
        for i, (source, target) in enumerate(
            ((ctx_hbm, ctx_ref), (logged_hbm, logged_ref), (policy_hbm, policy_ref))
        )
    ]
    for move in moves:
        move.start()
    for move in moves:
        move.wait()
    logged = jnp.concatenate(features(logged_ref[...]), axis=0)
    acts = policy_ref[...]
    codes = jnp.concatenate([acts >> 9, (acts & 511) - 256], axis=0).astype(f32)
    small = jnp.concatenate([logged, codes], axis=0).astype(bf16)
    ctx = ctx_ref[...]
    for i in range(PLANES):
        plane_ref[i, :TILE, :] = ctx
        plane_ref[i, TILE:, :] = small
    for i in range(COLUMNS):
        column_ref[i, :TILE, :] = ctx
        column_ref[i, TILE:, :] = small[:NACT]


def policy_kernel(own_ref, other_ref, policy_ref):
    for half, ref in enumerate((own_ref, other_ref)):
        for j in range(PLANES):
            codes = ref[j, CODE_AT:ROWS, :].astype(f32).astype(i32)
            acts = (codes[:NPOL] << 9) + codes[NPOL:] + 256
            feats = jnp.concatenate(features(acts), axis=0).astype(bf16)
            policy_ref[:, (2 * j + half) * TILE : (2 * j + half + 1) * TILE] = feats


SCALE = math.log2(math.e) / D
CHUNK = 2


def first_kernel(place_ref, own_ref, other_ref, right_ref, policy_ref, kernel_ref, sums_ref, squares, acc):
    for b in range(COLUMNS):
        x = right_ref[b, :TILE, :].astype(f32)
        total = jnp.sum(x * x, axis=1, keepdims=True) * SCALE
        squares[:, b * TILE : (b + 1) * TILE] = jnp.transpose(jnp.broadcast_to(total, (TILE, TILE)))[:8]
    acc[...] = jnp.zeros_like(acc)

    def rows_of(step, carry):
        for piece in range(CHUNK):
            for half, ref in enumerate((own_ref, other_ref)):
                j = step * CHUNK + piece
                rows = ref[j, :TILE, :]
                wide = rows.astype(f32)
                row_sq = jnp.sum(wide * wide, axis=1, keepdims=True) * SCALE
                at = pl.multiple_of(step * (2 * CHUNK * TILE), 2 * CHUNK * TILE) + (2 * piece + half) * TILE
                for b in range(0, COLUMNS, 2):
                    cols = right_ref[b : b + 2, :TILE, :].reshape(2 * TILE, D)
                    inner = lax.dot_general(rows, cols, (((1,), (1,)), ((), ())), preferred_element_type=f32)
                    span = slice(b * TILE, (b + 2) * TILE)
                    expo = (2.0 * SCALE) * inner - row_sq - squares[0:1, span]
                    kernel_ref[pl.ds(at, TILE), span] = jnp.exp2(expo).astype(bf16)
        start = pl.multiple_of(step * (2 * CHUNK * TILE), 2 * CHUNK * TILE)
        whole = pl.ds(start, 2 * CHUNK * TILE)
        acc[...] += jnp.dot(policy_ref[:, whole], kernel_ref[whole, :], preferred_element_type=f32)
        return carry

    lax.fori_loop(0, PLANES // CHUNK, rows_of, 0)
    for b in range(COLUMNS):
        chosen = right_ref[b, FEAT_AT : FEAT_AT + NACT, :].astype(f32)
        total = jnp.zeros((NPOL, TILE), f32)
        for c in range(NACT):
            total += acc[c * NPOL : (c + 1) * NPOL, b * TILE : (b + 1) * TILE] * chosen[c : c + 1]
        for peer in range(COLUMNS):
            sums_ref[peer, b] = total


def second_kernel(place_ref, kernel_ref, parts_ref, right_ref, own_ref, other_ref, image_ref, side_ref, matched):
    factor = NACT / (TILE * LEFT * COLUMNS)
    for b in range(COLUMNS):
        total = parts_ref[0, b]
        for peer in range(1, COLUMNS):
            total += parts_ref[peer, b]
        total = total * factor
        side_ref[b] = total
        low = total.astype(bf16).astype(f32)
        chosen = right_ref[b, FEAT_AT : FEAT_AT + NACT, :].astype(f32)
        made = jnp.concatenate([chosen[c : c + 1] * low for c in range(NACT)], axis=0)
        matched[:, b * TILE : (b + 1) * TILE] = made.astype(bf16)
    core = place_ref[0]

    def rows_of(step, carry):
        start = pl.multiple_of(step * (2 * CHUNK * TILE), 2 * CHUNK * TILE)
        block = kernel_ref[pl.ds(start, 2 * CHUNK * TILE), :]
        out = lax.dot_general(matched[...], block, (((1,), (1,)), ((), ())), preferred_element_type=f32)
        for piece in range(CHUNK):
            j = step * CHUNK + piece
            for half, ref in enumerate((own_ref, other_ref)):
                chosen = ref[j, FEAT_AT : FEAT_AT + NACT, :].astype(f32)
                at = (2 * piece + half) * TILE
                total = jnp.zeros((NPOL, TILE), f32)
                for c in range(NACT):
                    total += out[c * NPOL : (c + 1) * NPOL, at : at + TILE] * chosen[c : c + 1]
                image_ref[2 * j + jnp.where(core == half, 0, 1)] = total * factor
        return carry

    lax.fori_loop(0, PLANES // CHUNK, rows_of, 0)


def third_kernel(place_ref, parts_ref, side_ref, rewards_ref, image_ref, own_ref, sums_ref):
    total = parts_ref[0]
    for i in range(1, LEFT):
        total += parts_ref[i]
    side = side_ref[place_ref[1]]
    image = total + ridge * side
    image_ref[...] = image
    own_ref[...] = side
    lane = lax.broadcasted_iota(i32, (NPOL, TILE), 1)
    row = lax.broadcasted_iota(i32, (NPOL, TILE), 0)
    spread = jnp.zeros((NPOL, TILE), f32)
    for k, value in enumerate((side * side, side * image, rewards_ref[...] * side)):
        spread = jnp.where(lane == row + k * NPOL, jnp.sum(value, axis=1, keepdims=True), spread)
    flat = jnp.sum(spread, axis=0, keepdims=True)
    sums_ref[...] = jnp.broadcast_to(flat, sums_ref.shape)


def last_kernel(sums_ref, image_ref, side_ref, weights_ref, residual_ref, values_ref):
    count = sums_ref.shape[0]
    total = jnp.sum(sums_ref[...], axis=0, keepdims=True)
    lane = lax.broadcasted_iota(i32, (NPOL, TILE), 1)
    row = lax.broadcasted_iota(i32, (NPOL, TILE), 0)
    wide = jnp.broadcast_to(total, (NPOL, TILE))

    def pick(k):
        return jnp.sum(jnp.where(lane == row + k * NPOL, wide, 0.0), axis=1, keepdims=True)

    alpha = pick(0) / pick(1)
    side = side_ref[...]
    weights_ref[...] = alpha * side
    residual_ref[...] = side - alpha * image_ref[...]
    values = alpha * pick(2) / (TILE * count)
    values_ref[...] = jnp.sum(jnp.where(lane == row, values, 0.0), axis=0, keepdims=True)[:, :NPOL]


def params(limit=32 * MIB):
    return pltpu.CompilerParams(vmem_limit_bytes=limit)


def exchange(value, axes):
    return lax.all_to_all(value, axes, 0, 0)


def on_device(contexts, logged_actions, policy_actions, rewards):
    core = lax.axis_index("core")
    column = lax.axis_index(COLUMN)
    place = jnp.stack([core, column]).astype(i32)
    sds = jax.ShapeDtypeStruct
    vmem = pl.BlockSpec(memory_space=pltpu.VMEM)
    smem = pl.BlockSpec(memory_space=pltpu.SMEM)

    plane_send, column_send = pl.pallas_call(
        prepare,
        in_specs=[pl.BlockSpec(memory_space=pl.ANY)] * 3,
        out_shape=(sds((PLANES, ROWS, D), bf16), sds((COLUMNS, RIGHT_ROWS, D), bf16)),
        scratch_shapes=[
            pltpu.VMEM((TILE, D), bf16),
            pltpu.VMEM((1, TILE), i32),
            pltpu.VMEM((NPOL, TILE), i32),
            pltpu.SemaphoreType.DMA((3,)),
        ],
        compiler_params=params(60 * MIB),
    )(contexts, logged_actions.reshape(1, TILE), policy_actions.T)
    own = exchange(plane_send, PLANE)
    other = lax.ppermute(own, "core", [(0, 1), (1, 0)])
    right = exchange(column_send, COLUMN)

    width = COLUMNS * TILE
    policy = pl.pallas_call(
        policy_kernel,
        out_shape=sds((TILE, LEFT * TILE), bf16),
        cost_estimate=pl.CostEstimate(flops=60_000_000, bytes_accessed=2_000_000, transcendentals=0),
        compiler_params=params(),
    )(own, other)
    kernel, first = pl.pallas_call(
        first_kernel,
        in_specs=[smem] + [vmem] * 4,
        out_shape=(sds((LEFT * TILE, width), bf16), sds((COLUMNS, COLUMNS, NPOL, TILE), f32)),
        scratch_shapes=[pltpu.VMEM((8, width), f32), pltpu.VMEM((TILE, width), f32)],
        compiler_params=params(),
    )(place, own, other, right, policy)
    parts = exchange(first, COLUMN)
    image_parts, side = pl.pallas_call(
        second_kernel,
        in_specs=[smem] + [vmem] * 5,
        out_shape=(sds((LEFT, NPOL, TILE), f32), sds((COLUMNS, NPOL, TILE), f32)),
        scratch_shapes=[pltpu.VMEM((TILE, width), bf16)],
        compiler_params=params(),
    )(place, kernel, parts, right, own, other)
    image_parts = exchange(image_parts, PLANE + ("core",))

    count = LEFT * COLUMNS
    image, own_side, sums = pl.pallas_call(
        third_kernel,
        in_specs=[smem, vmem, vmem, vmem],
        out_shape=(sds((NPOL, TILE), f32), sds((NPOL, TILE), f32), sds((count, TILE), f32)),
        compiler_params=params(),
    )(place, image_parts, side, rewards.reshape(1, TILE))
    sums = exchange(sums.reshape(count, 1, TILE), EVERY).reshape(count, TILE)
    weights, residual, values = pl.pallas_call(
        last_kernel,
        out_shape=(sds((NPOL, TILE), f32), sds((NPOL, TILE), f32), sds((1, NPOL), f32)),
        compiler_params=params(),
    )(sums, image, own_side)
    return weights.T, residual.T, values.reshape(NPOL)


def solution(mesh):
    fine = Mesh(mesh.devices.reshape([size for _, size in SIZES]), EVERY)
    return jax.shard_map(
        on_device,
        mesh=fine,
        in_specs=(P(EVERY, None), P(EVERY), P(EVERY, None), P(EVERY)),
        out_specs=(P(EVERY, None), P(EVERY, None), P()),
        check_vma=False,
    )
```

```python
import math

import jax
import jax.numpy as jnp
from jax import lax
from jax.experimental import pallas as pl
from jax.experimental.pallas import tpu as pltpu
from jax.sharding import Mesh
from jax.sharding import PartitionSpec as P

NPOL = 8
NACT = 16
CATALOG = 131042
D = 128
TILE = 128

ridge = 0.1
stride_base = 1009
phase_step = 0.37
two_pi = 2.0 * math.pi

SIZES = (("z_hi", 2), ("x", 4), ("z_lo", 4), ("y", 4), ("core", 2))
EVERY = tuple(name for name, _ in SIZES)
PLANE = ("x", "y")
COLUMN = ("z_hi", "z_lo")
PLANES = 16
COLUMNS = 8
LEFT = 2 * PLANES
ROWS = 160
FEAT_AT, CODE_AT = 128, 144
RIGHT_ROWS = 144

f32, bf16, i32 = jnp.float32, jnp.bfloat16, jnp.int32
MIB = 1 << 20


def wrap(product):
    guess = (product.astype(f32) * (1.0 / CATALOG)).astype(i32)
    left = product - guess * CATALOG
    left = jnp.where(left < 0, left + CATALOG, left)
    return jnp.where(left >= CATALOG, left - CATALOG, left)


def cos_sin(turn):
    eighth = (turn.astype(f32) * (4.0 / CATALOG) + 0.5).astype(i32)
    rest = 4 * turn - eighth * CATALOG
    t = rest.astype(f32) * (two_pi / 4 / CATALOG)
    u = t * t
    s = t * (1.0 + u * (-1.0 / 6 + u * (1.0 / 120 + u * (-1.0 / 5040 + u * (1.0 / 362880)))))
    c = 1.0 + u * (-0.5 + u * (1.0 / 24 + u * (-1.0 / 720 + u * (1.0 / 40320))))
    swap = (eighth == 1) | (eighth == 3)
    a = jnp.where(swap, s, c)
    b = jnp.where(swap, c, s)
    a = jnp.where((eighth == 1) | (eighth == 2), -a, a)
    b = jnp.where((eighth == 2) | (eighth == 3), -b, b)
    return a, b


def features(chosen):
    amp = math.sqrt(2.0 / NACT)
    c0, s0 = cos_sin(chosen)
    cz, sz = cos_sin(wrap(chosen * stride_base))
    pc, ps = math.cos(phase_step), math.sin(phase_step)
    zr = cz * pc - sz * ps
    zi = cz * ps + sz * pc
    wr, wi = c0 * amp, s0 * amp
    out = [jnp.full(chosen.shape, 1.0 / math.sqrt(NACT), f32)]
    for _ in range(1, NACT):
        wr, wi = wr * zr - wi * zi, wr * zi + wi * zr
        out.append(wr)
    return out


def prepare(ctx_hbm, logged_hbm, policy_hbm, plane_ref, mine_ref, ctx_ref, logged_ref, policy_ref, sems):
    moves = [
        pltpu.make_async_copy(source, target, sems.at[i])
        for i, (source, target) in enumerate(
            ((ctx_hbm, ctx_ref), (logged_hbm, logged_ref), (policy_hbm, policy_ref))
        )
    ]
    for move in moves:
        move.start()
    for move in moves:
        move.wait()
    logged = jnp.concatenate(features(logged_ref[...]), axis=0)
    acts = policy_ref[...]
    codes = jnp.concatenate([acts >> 9, (acts & 511) - 256], axis=0).astype(f32)
    small = jnp.concatenate([logged, codes], axis=0).astype(bf16)
    ctx = ctx_ref[...]
    for i in range(PLANES):
        plane_ref[i, :TILE, :] = ctx
        plane_ref[i, TILE:, :] = small
    mine_ref[:TILE, :] = ctx
    mine_ref[TILE:, :] = small[:NACT]


def policy_kernel(own_ref, other_ref, policy_ref):
    for half, ref in enumerate((own_ref, other_ref)):
        for j in range(PLANES):
            codes = ref[j, CODE_AT:ROWS, :].astype(f32).astype(i32)
            acts = (codes[:NPOL] << 9) + codes[NPOL:] + 256
            feats = jnp.concatenate(features(acts), axis=0).astype(bf16)
            policy_ref[:, (2 * j + half) * TILE : (2 * j + half + 1) * TILE] = feats


SCALE = math.log2(math.e) / D
CHUNK = 8
BESIDE = 5
SPAN = 2 * CHUNK * TILE


def home(place_ref, shift):
    return lax.rem(place_ref[1] + (COLUMNS - shift), COLUMNS)


def first_kernel(place_ref, own_ref, other_ref, policy_ref, *refs):
    right_refs = (own_ref.at[place_ref[2]], *refs[: COLUMNS - 1])
    kernel_ref, sums_ref, squares, acc, cols = refs[COLUMNS - 1 :]
    for b, right_ref in enumerate(right_refs):
        x = right_ref[:TILE, :]
        cols[b * TILE : (b + 1) * TILE, :] = x
        x = x.astype(f32)
        total = jnp.sum(x * x, axis=1, keepdims=True) * SCALE
        squares[:, b * TILE : (b + 1) * TILE] = jnp.transpose(jnp.broadcast_to(total, (TILE, TILE)))[:8]
    acc[...] = jnp.zeros_like(acc)
    for step in range(PLANES // CHUNK):
        tiles = [ref[j, :TILE, :] for j in range(step * CHUNK, (step + 1) * CHUNK) for ref in (own_ref, other_ref)]
        rows = jnp.concatenate(tiles, axis=0)
        wide = rows.astype(f32)
        row_sq = jnp.sum(wide * wide, axis=1, keepdims=True) * SCALE
        whole = slice(step * SPAN, (step + 1) * SPAN)
        for b in range(0, COLUMNS, 2):
            span = slice(b * TILE, (b + 2) * TILE)
            inner = lax.dot_general(rows, cols[span, :], (((1,), (1,)), ((), ())), preferred_element_type=f32)
            expo = (2.0 * SCALE) * inner - row_sq - squares[0:1, span]
            kernel_ref[whole, span] = jnp.exp2(expo).astype(bf16)
        acc[...] += jnp.dot(policy_ref[:, whole], kernel_ref[whole, :], preferred_element_type=f32)
    for b, right_ref in enumerate(right_refs):
        chosen = right_ref[FEAT_AT : FEAT_AT + NACT, :].astype(f32)
        total = jnp.zeros((NPOL, TILE), f32)
        for c in range(NACT):
            total += acc[c * NPOL : (c + 1) * NPOL, b * TILE : (b + 1) * TILE] * chosen[c : c + 1]
        at = home(place_ref, b)
        for peer in range(COLUMNS):
            sums_ref[peer, at] = total


def second_kernel(place_ref, kernel_ref, parts_ref, own_ref, other_ref, *refs):
    right_refs = (own_ref.at[place_ref[2]], *refs[: COLUMNS - 1])
    image_ref, side_ref, matched = refs[COLUMNS - 1 :]
    factor = NACT / (TILE * LEFT * COLUMNS)
    for b, right_ref in enumerate(right_refs):
        at = home(place_ref, b)
        total = parts_ref[0, at]
        for peer in range(1, COLUMNS):
            total += parts_ref[peer, at]
        total = total * factor
        if b == 0:
            side_ref[...] = total
        low = total.astype(bf16).astype(f32)
        chosen = right_ref[FEAT_AT : FEAT_AT + NACT, :].astype(f32)
        made = jnp.concatenate([chosen[c : c + 1] * low for c in range(NACT)], axis=0)
        matched[b * TILE : (b + 1) * TILE, :] = jnp.transpose(made).astype(bf16)
    core = place_ref[0]
    for step in range(PLANES // CHUNK):
        block = kernel_ref[step * SPAN : (step + 1) * SPAN, :]
        out = jnp.transpose(jnp.dot(block, matched[...], preferred_element_type=f32))
        for j in range(step * CHUNK, (step + 1) * CHUNK):
            for half, ref in enumerate((own_ref, other_ref)):
                chosen = ref[j, FEAT_AT : FEAT_AT + NACT, :].astype(f32)
                at = (2 * (j - step * CHUNK) + half) * TILE
                total = jnp.zeros((NPOL, TILE), f32)
                for c in range(NACT):
                    total += out[c * NPOL : (c + 1) * NPOL, at : at + TILE] * chosen[c : c + 1]
                image_ref[2 * j + jnp.where(core == half, 0, 1)] = total * factor


def third_kernel(parts_ref, side_ref, rewards_ref, image_ref, sums_ref):
    total = parts_ref[0]
    for i in range(1, LEFT):
        total += parts_ref[i]
    side = side_ref[...]
    image = total + ridge * side
    image_ref[...] = image
    lane = lax.broadcasted_iota(i32, (NPOL, TILE), 1)
    row = lax.broadcasted_iota(i32, (NPOL, TILE), 0)
    spread = jnp.zeros((NPOL, TILE), f32)
    for k, value in enumerate((side * side, side * image, rewards_ref[...] * side)):
        spread = jnp.where(lane == row + k * NPOL, jnp.sum(value, axis=1, keepdims=True), spread)
    flat = jnp.sum(spread, axis=0, keepdims=True)
    sums_ref[...] = jnp.broadcast_to(flat, sums_ref.shape)


def last_kernel(sums_ref, image_ref, side_ref, weights_ref, residual_ref, values_ref):
    count = sums_ref.shape[0]
    total = jnp.sum(sums_ref[...], axis=0, keepdims=True)
    lane = lax.broadcasted_iota(i32, (NPOL, TILE), 1)
    row = lax.broadcasted_iota(i32, (NPOL, TILE), 0)
    wide = jnp.broadcast_to(total, (NPOL, TILE))

    def pick(k):
        return jnp.sum(jnp.where(lane == row + k * NPOL, wide, 0.0), axis=1, keepdims=True)

    alpha = pick(0) / pick(1)
    side = side_ref[...]
    weights_ref[...] = alpha * side
    residual_ref[...] = side - alpha * image_ref[...]
    values = alpha * pick(2) / (TILE * count)
    values_ref[...] = jnp.sum(jnp.where(lane == row, values, 0.0), axis=0, keepdims=True)[:, :NPOL]


def params(limit=32 * MIB):
    return pltpu.CompilerParams(vmem_limit_bytes=limit)


def exchange(value, axes):
    return lax.all_to_all(value, axes, 0, 0)


def on_device(contexts, logged_actions, policy_actions, rewards):
    core = lax.axis_index("core")
    column = lax.axis_index(COLUMN)
    place = jnp.stack([core, column, lax.axis_index(PLANE)]).astype(i32)
    sds = jax.ShapeDtypeStruct
    vmem = pl.BlockSpec(memory_space=pltpu.VMEM)
    smem = pl.BlockSpec(memory_space=pltpu.SMEM)

    plane_send, mine = pl.pallas_call(
        prepare,
        in_specs=[pl.BlockSpec(memory_space=pl.ANY)] * 3,
        out_shape=(sds((PLANES, ROWS, D), bf16), sds((RIGHT_ROWS, D), bf16)),
        scratch_shapes=[
            pltpu.VMEM((TILE, D), bf16),
            pltpu.VMEM((1, TILE), i32),
            pltpu.VMEM((NPOL, TILE), i32),
            pltpu.SemaphoreType.DMA((3,)),
        ],
        compiler_params=params(60 * MIB),
    )(contexts, logged_actions.reshape(1, TILE), policy_actions.T)
    ring = lambda shift: [(i, (i + shift) % COLUMNS) for i in range(COLUMNS)]
    right = [lax.ppermute(mine, COLUMN, ring(shift)) for shift in range(1, COLUMNS)]
    own, *right[:BESIDE] = lax.optimization_barrier((exchange(plane_send, PLANE), *right[:BESIDE]))
    other = lax.ppermute(own, "core", [(0, 1), (1, 0)])

    width = COLUMNS * TILE
    policy = pl.pallas_call(
        policy_kernel,
        out_shape=sds((TILE, LEFT * TILE), bf16),
        cost_estimate=pl.CostEstimate(flops=60_000_000, bytes_accessed=2_000_000, transcendentals=0),
        compiler_params=params(),
    )(own, other)
    kernel, first = pl.pallas_call(
        first_kernel,
        in_specs=[smem] + [vmem] * (2 + COLUMNS),
        out_shape=(sds((LEFT * TILE, width), bf16), sds((COLUMNS, COLUMNS, NPOL, TILE), f32)),
        scratch_shapes=[pltpu.VMEM((8, width), f32), pltpu.VMEM((TILE, width), f32), pltpu.VMEM((width, D), bf16)],
        compiler_params=params(),
    )(place, own, other, policy, *right)
    parts = exchange(first, COLUMN)
    image_parts, side = pl.pallas_call(
        second_kernel,
        in_specs=[smem] + [vmem] * (3 + COLUMNS),
        out_shape=(sds((LEFT, NPOL, TILE), f32), sds((NPOL, TILE), f32)),
        scratch_shapes=[pltpu.VMEM((width, TILE), bf16)],
        compiler_params=params(),
    )(place, kernel, parts, own, other, *right)
    image_parts = exchange(image_parts, PLANE + ("core",))

    count = LEFT * COLUMNS
    image, sums = pl.pallas_call(
        third_kernel,
                out_shape=(sds((NPOL, TILE), f32), sds((count, TILE), f32)),
        compiler_params=params(),
    )(image_parts, side, rewards.reshape(1, TILE))
    sums = exchange(sums.reshape(count, 1, TILE), EVERY).reshape(count, TILE)
    weights, residual, values = pl.pallas_call(
        last_kernel,
        out_shape=(sds((NPOL, TILE), f32), sds((NPOL, TILE), f32), sds((1, NPOL), f32)),
        compiler_params=params(),
    )(sums, image, side)
    return weights.T, residual.T, values.reshape(NPOL)


def solution(mesh):
    fine = Mesh(mesh.devices.reshape([size for _, size in SIZES]), EVERY)
    return jax.shard_map(
        on_device,
        mesh=fine,
        in_specs=(P(EVERY, None), P(EVERY), P(EVERY, None), P(EVERY)),
        out_specs=(P(EVERY, None), P(EVERY, None), P()),
        check_vma=False,
    )
```

```python
import math

import jax
import jax.numpy as jnp
from jax import lax
from jax.experimental import pallas as pl
from jax.experimental.pallas import tpu as pltpu
from jax.sharding import Mesh
from jax.sharding import PartitionSpec as P

NPOL = 8
NACT = 16
CATALOG = 131042
D = 128
TILE = 128

ridge = 0.1
stride_base = 1009
phase_step = 0.37
two_pi = 2.0 * math.pi

SIZES = (("z_hi", 2), ("x", 4), ("z_lo", 4), ("y", 4), ("core", 2))
EVERY = tuple(name for name, _ in SIZES)
PLANE = ("x", "y")
COLUMN = ("z_hi", "z_lo")
PLANES = 16
COLUMNS = 8
LEFT = 2 * PLANES
ROWS = 160
FEAT_AT, CODE_AT = 128, 144
RIGHT_ROWS = 144

f32, bf16, i32 = jnp.float32, jnp.bfloat16, jnp.int32
MIB = 1 << 20


def wrap(product):
    guess = (product.astype(f32) * (1.0 / CATALOG)).astype(i32)
    left = product - guess * CATALOG
    left = jnp.where(left < 0, left + CATALOG, left)
    return jnp.where(left >= CATALOG, left - CATALOG, left)


def cos_sin(turn):
    eighth = (turn.astype(f32) * (4.0 / CATALOG) + 0.5).astype(i32)
    rest = 4 * turn - eighth * CATALOG
    t = rest.astype(f32) * (two_pi / 4 / CATALOG)
    u = t * t
    s = t * (1.0 + u * (-1.0 / 6 + u * (1.0 / 120 + u * (-1.0 / 5040 + u * (1.0 / 362880)))))
    c = 1.0 + u * (-0.5 + u * (1.0 / 24 + u * (-1.0 / 720 + u * (1.0 / 40320))))
    swap = (eighth == 1) | (eighth == 3)
    a = jnp.where(swap, s, c)
    b = jnp.where(swap, c, s)
    a = jnp.where((eighth == 1) | (eighth == 2), -a, a)
    b = jnp.where((eighth == 2) | (eighth == 3), -b, b)
    return a, b


def features(chosen):
    amp = math.sqrt(2.0 / NACT)
    c0, s0 = cos_sin(chosen)
    cz, sz = cos_sin(wrap(chosen * stride_base))
    pc, ps = math.cos(phase_step), math.sin(phase_step)
    zr = cz * pc - sz * ps
    zi = cz * ps + sz * pc
    wr, wi = c0 * amp, s0 * amp
    out = [jnp.full(chosen.shape, 1.0 / math.sqrt(NACT), f32)]
    for _ in range(1, NACT):
        wr, wi = wr * zr - wi * zi, wr * zi + wi * zr
        out.append(wr)
    return out


def prepare(ctx_hbm, logged_hbm, policy_hbm, plane_ref, mine_ref, ctx_ref, logged_ref, policy_ref, sems):
    moves = [
        pltpu.make_async_copy(source, target, sems.at[i])
        for i, (source, target) in enumerate(
            ((ctx_hbm, ctx_ref), (logged_hbm, logged_ref), (policy_hbm, policy_ref))
        )
    ]
    for move in moves:
        move.start()
    for move in moves:
        move.wait()
    logged = jnp.concatenate(features(logged_ref[...]), axis=0)
    acts = policy_ref[...]
    codes = jnp.concatenate([acts >> 9, (acts & 511) - 256], axis=0).astype(f32)
    small = jnp.concatenate([logged, codes], axis=0).astype(bf16)
    ctx = ctx_ref[...]
    for i in range(PLANES):
        plane_ref[i, :TILE, :] = ctx
        plane_ref[i, TILE:, :] = small
    mine_ref[:TILE, :] = ctx
    mine_ref[TILE:, :] = small[:NACT]


def pieces(total):
    high = total.astype(bf16).astype(f32)
    rest = total - high
    middle = rest.astype(bf16).astype(f32)
    return high, middle, rest - middle


def lanes():
    return lax.broadcasted_iota(i32, (TILE, TILE), 1)


def policy_kernel(own_ref, other_ref, policy_ref, extra_ref):
    lane = lanes()
    for half, ref in enumerate((own_ref, other_ref)):
        for j in range(PLANES):
            at = 2 * j + half
            codes = ref[j, CODE_AT:ROWS, :].astype(f32).astype(i32)
            acts = (codes[:NPOL] << 9) + codes[NPOL:] + 256
            feats = jnp.concatenate(features(acts), axis=0).astype(bf16)
            policy_ref[:, at * TILE : (at + 1) * TILE] = feats
            wide = ref[j, :TILE, :].astype(f32)
            high, middle, low = pieces(jnp.sum(wide * wide, axis=1, keepdims=True))
            extra = jnp.where(lane == 0, high, jnp.where(lane == 1, middle, jnp.where(lane == 2, low, 1.0)))
            extra_ref[at] = extra.astype(bf16)


SCALE = math.log2(math.e) / D
CHUNK = 8
BESIDE = 3
SPAN = 2 * CHUNK * TILE


def home(place_ref, shift):
    return lax.rem(place_ref[1] + (COLUMNS - shift), COLUMNS)


def block(left_refs, right_refs, kernel_ref, acc, cols):
    own_ref, other_ref, policy_ref, extra_ref = left_refs
    lane = lanes()
    for b, right_ref in enumerate(right_refs):
        here = slice(b * TILE, (b + 1) * TILE)
        x = right_ref[:TILE, :].astype(f32)
        high, middle, low = pieces(jnp.sum(x * x, axis=1, keepdims=True))
        extra = jnp.where(lane < 3, -1.0, 0.0)
        for at, piece in ((3, high), (4, middle), (5, low)):
            extra = jnp.where(lane == at, -piece, extra)
        cols[here, :D] = (2.0 * x).astype(bf16)
        cols[here, D:] = extra.astype(bf16)
    width = len(right_refs) * TILE
    wide = 2 * TILE
    for step in range(PLANES // CHUNK):
        rows = jnp.concatenate(
            [
                jnp.concatenate([ref[j, :TILE, :], extra_ref[2 * j + half]], axis=1)
                for j in range(step * CHUNK, (step + 1) * CHUNK)
                for half, ref in enumerate((own_ref, other_ref))
            ],
            axis=0,
        )
        whole = slice(step * SPAN, (step + 1) * SPAN)
        for at in range(0, width, wide):
            span = slice(at, at + wide)
            expo = lax.dot_general(rows, cols[span, :], (((1,), (1,)), ((), ())), preferred_element_type=f32)
            kernel_ref[whole, span] = jnp.exp2(SCALE * expo).astype(bf16)
        term = jnp.dot(policy_ref[:, whole], kernel_ref[whole, :], preferred_element_type=f32)
        if step:
            term += acc[...]
        acc[...] = term
    sums = []
    for b, right_ref in enumerate(right_refs):
        chosen = right_ref[FEAT_AT : FEAT_AT + NACT, :].astype(f32)
        total = jnp.zeros((NPOL, TILE), f32)
        for c in range(NACT):
            total += acc[c * NPOL : (c + 1) * NPOL, b * TILE : (b + 1) * TILE] * chosen[c : c + 1]
        sums.append(total)
    return sums


def first_half(place_ref, own_ref, other_ref, policy_ref, extra_ref, *refs):
    right_refs = (own_ref.at[place_ref[2]], *refs[:BESIDE])
    kernel_ref, sums_ref, acc, cols = refs[BESIDE:]
    for b, total in enumerate(block((own_ref, other_ref, policy_ref, extra_ref), right_refs, kernel_ref, acc, cols)):
        sums_ref[b] = total


def second_half(place_ref, own_ref, other_ref, policy_ref, extra_ref, done_ref, *refs):
    right_refs = refs[: COLUMNS - 1 - BESIDE]
    kernel_ref, sums_ref, acc, cols = refs[COLUMNS - 1 - BESIDE :]
    totals = block((own_ref, other_ref, policy_ref, extra_ref), right_refs, kernel_ref, acc, cols)
    totals = [done_ref[b] for b in range(BESIDE + 1)] + totals
    for b, total in enumerate(totals):
        at = home(place_ref, b)
        for peer in range(COLUMNS):
            sums_ref[peer, at] = total


def second_kernel(place_ref, near_ref, far_ref, parts_ref, own_ref, other_ref, *refs):
    right_refs = (own_ref.at[place_ref[2]], *refs[: COLUMNS - 1])
    image_ref, side_ref, matched = refs[COLUMNS - 1 :]
    factor = NACT / (TILE * LEFT * COLUMNS)
    for b, right_ref in enumerate(right_refs):
        at = home(place_ref, b)
        total = parts_ref[0, at]
        for peer in range(1, COLUMNS):
            total += parts_ref[peer, at]
        total = total * factor
        if b == 0:
            side_ref[...] = total
        low = total.astype(bf16).astype(f32)
        chosen = right_ref[FEAT_AT : FEAT_AT + NACT, :].astype(f32)
        made = jnp.concatenate([chosen[c : c + 1] * low for c in range(NACT)], axis=0)
        matched[b * TILE : (b + 1) * TILE, :] = jnp.transpose(made).astype(bf16)
    core = place_ref[0]
    cut = (BESIDE + 1) * TILE
    for step in range(PLANES // CHUNK):
        whole = slice(step * SPAN, (step + 1) * SPAN)
        out = jnp.dot(near_ref[whole, :], matched[:cut, :], preferred_element_type=f32)
        out += jnp.dot(far_ref[whole, :], matched[cut:, :], preferred_element_type=f32)
        out = jnp.transpose(out)
        for j in range(step * CHUNK, (step + 1) * CHUNK):
            for half, ref in enumerate((own_ref, other_ref)):
                chosen = ref[j, FEAT_AT : FEAT_AT + NACT, :].astype(f32)
                at = (2 * (j - step * CHUNK) + half) * TILE
                total = jnp.zeros((NPOL, TILE), f32)
                for c in range(NACT):
                    total += out[c * NPOL : (c + 1) * NPOL, at : at + TILE] * chosen[c : c + 1]
                image_ref[2 * j + jnp.where(core == half, 0, 1)] = total * factor


def third_kernel(parts_ref, side_ref, rewards_ref, image_ref, sums_ref):
    total = parts_ref[0]
    for i in range(1, LEFT):
        total += parts_ref[i]
    side = side_ref[...]
    image = total + ridge * side
    image_ref[...] = image
    lane = lax.broadcasted_iota(i32, (NPOL, TILE), 1)
    row = lax.broadcasted_iota(i32, (NPOL, TILE), 0)
    spread = jnp.zeros((NPOL, TILE), f32)
    for k, value in enumerate((side * side, side * image, rewards_ref[...] * side)):
        spread = jnp.where(lane == row + k * NPOL, jnp.sum(value, axis=1, keepdims=True), spread)
    flat = jnp.sum(spread, axis=0, keepdims=True)
    sums_ref[...] = jnp.broadcast_to(flat, sums_ref.shape)


def last_kernel(sums_ref, image_ref, side_ref, weights_ref, residual_ref, values_ref):
    count = sums_ref.shape[0]
    total = jnp.sum(sums_ref[...], axis=0, keepdims=True)
    lane = lax.broadcasted_iota(i32, (NPOL, TILE), 1)
    row = lax.broadcasted_iota(i32, (NPOL, TILE), 0)
    wide = jnp.broadcast_to(total, (NPOL, TILE))

    def pick(k):
        return jnp.sum(jnp.where(lane == row + k * NPOL, wide, 0.0), axis=1, keepdims=True)

    alpha = pick(0) / pick(1)
    side = side_ref[...]
    weights_ref[...] = alpha * side
    residual_ref[...] = side - alpha * image_ref[...]
    values = alpha * pick(2) / (TILE * count)
    values_ref[...] = jnp.sum(jnp.where(lane == row, values, 0.0), axis=0, keepdims=True)[:, :NPOL]


def params(limit=32 * MIB):
    return pltpu.CompilerParams(vmem_limit_bytes=limit)


def exchange(value, axes):
    return lax.all_to_all(value, axes, 0, 0)


def on_device(contexts, logged_actions, policy_actions, rewards):
    core = lax.axis_index("core")
    column = lax.axis_index(COLUMN)
    place = jnp.stack([core, column, lax.axis_index(PLANE)]).astype(i32)
    sds = jax.ShapeDtypeStruct
    vmem = pl.BlockSpec(memory_space=pltpu.VMEM)
    smem = pl.BlockSpec(memory_space=pltpu.SMEM)

    plane_send, mine = pl.pallas_call(
        prepare,
        in_specs=[pl.BlockSpec(memory_space=pl.ANY)] * 3,
        out_shape=(sds((PLANES, ROWS, D), bf16), sds((RIGHT_ROWS, D), bf16)),
        scratch_shapes=[
            pltpu.VMEM((TILE, D), bf16),
            pltpu.VMEM((1, TILE), i32),
            pltpu.VMEM((NPOL, TILE), i32),
            pltpu.SemaphoreType.DMA((3,)),
        ],
        compiler_params=params(60 * MIB),
    )(contexts, logged_actions.reshape(1, TILE), policy_actions.T)
    ring = lambda shift: [(i, (i + shift) % COLUMNS) for i in range(COLUMNS)]
    right = [lax.ppermute(mine, COLUMN, ring(shift)) for shift in range(1, COLUMNS)]
    own, *right[:BESIDE] = lax.optimization_barrier((exchange(plane_send, PLANE), *right[:BESIDE]))
    other = lax.ppermute(own, "core", [(0, 1), (1, 0)])

    policy, extra = pl.pallas_call(
        policy_kernel,
        out_shape=(sds((TILE, LEFT * TILE), bf16), sds((LEFT, TILE, TILE), bf16)),
        cost_estimate=pl.CostEstimate(flops=60_000_000, bytes_accessed=3_000_000, transcendentals=0),
        compiler_params=params(),
    )(own, other)
    left = (place, own, other, policy, extra)
    rows = LEFT * TILE

    def cost(width):
        return pl.CostEstimate(
            flops=2 * rows * width * (2 * D + TILE), bytes_accessed=2 * rows * (width + 4 * D), transcendentals=rows * width
        )

    near, far = (BESIDE + 1) * TILE, (COLUMNS - 1 - BESIDE) * TILE
    scratch = lambda width: [pltpu.VMEM((TILE, width), f32), pltpu.VMEM((width, 2 * D), bf16)]
    near_block, done = pl.pallas_call(
        first_half,
        in_specs=[smem] + [vmem] * (4 + BESIDE),
        out_shape=(sds((rows, near), bf16), sds((BESIDE + 1, NPOL, TILE), f32)),
        scratch_shapes=scratch(near),
        cost_estimate=cost(near),
        compiler_params=params(),
    )(*left, *right[:BESIDE])
    far_block, first = pl.pallas_call(
        second_half,
        in_specs=[smem] + [vmem] * (4 + COLUMNS - BESIDE),
        out_shape=(sds((rows, far), bf16), sds((COLUMNS, COLUMNS, NPOL, TILE), f32)),
        scratch_shapes=scratch(far),
        cost_estimate=cost(far),
        compiler_params=params(),
    )(*left, done, *right[BESIDE:])
    parts = exchange(first, COLUMN)
    image_parts, side = pl.pallas_call(
        second_kernel,
        in_specs=[smem] + [vmem] * (4 + COLUMNS),
        out_shape=(sds((LEFT, NPOL, TILE), f32), sds((NPOL, TILE), f32)),
        scratch_shapes=[pltpu.VMEM((COLUMNS * TILE, TILE), bf16)],
        compiler_params=params(),
    )(place, near_block, far_block, parts, own, other, *right)
    image_parts = exchange(image_parts, PLANE + ("core",))

    count = LEFT * COLUMNS
    image, sums = pl.pallas_call(
        third_kernel,
                out_shape=(sds((NPOL, TILE), f32), sds((count, TILE), f32)),
        compiler_params=params(),
    )(image_parts, side, rewards.reshape(1, TILE))
    sums = exchange(sums.reshape(count, 1, TILE), EVERY).reshape(count, TILE)
    weights, residual, values = pl.pallas_call(
        last_kernel,
        out_shape=(sds((NPOL, TILE), f32), sds((NPOL, TILE), f32), sds((1, NPOL), f32)),
        compiler_params=params(),
    )(sums, image, side)
    return weights.T, residual.T, values.reshape(NPOL)


def solution(mesh):
    fine = Mesh(mesh.devices.reshape([size for _, size in SIZES]), EVERY)
    return jax.shard_map(
        on_device,
        mesh=fine,
        in_specs=(P(EVERY, None), P(EVERY), P(EVERY, None), P(EVERY)),
        out_specs=(P(EVERY, None), P(EVERY, None), P()),
        check_vma=False,
    )
```

```python
import math

import jax
import jax.numpy as jnp
from jax import lax
from jax.experimental import pallas as pl
from jax.experimental.pallas import tpu as pltpu
from jax.sharding import Mesh
from jax.sharding import PartitionSpec as P

NPOL = 8
NACT = 16
CATALOG = 131042
D = 128
TILE = 128

ridge = 0.1
stride_base = 1009
phase_step = 0.37
two_pi = 2.0 * math.pi

SIZES = (("z_hi", 2), ("x", 4), ("z_lo", 4), ("y", 4), ("core", 2))
EVERY = tuple(name for name, _ in SIZES)
PLANE = ("x", "y")
COLUMN = ("z_hi", "z_lo")
PLANES = 16
COLUMNS = 8
LEFT = 2 * PLANES
ROWS = 160
FEAT_AT, CODE_AT = 128, 144
RIGHT_ROWS = 144

f32, bf16, i32 = jnp.float32, jnp.bfloat16, jnp.int32
MIB = 1 << 20


def wrap(product):
    guess = (product.astype(f32) * (1.0 / CATALOG)).astype(i32)
    left = product - guess * CATALOG
    left = jnp.where(left < 0, left + CATALOG, left)
    return jnp.where(left >= CATALOG, left - CATALOG, left)


def cos_sin(turn):
    eighth = (turn.astype(f32) * (4.0 / CATALOG) + 0.5).astype(i32)
    rest = 4 * turn - eighth * CATALOG
    t = rest.astype(f32) * (two_pi / 4 / CATALOG)
    u = t * t
    s = t * (1.0 + u * (-1.0 / 6 + u * (1.0 / 120 + u * (-1.0 / 5040 + u * (1.0 / 362880)))))
    c = 1.0 + u * (-0.5 + u * (1.0 / 24 + u * (-1.0 / 720 + u * (1.0 / 40320))))
    swap = (eighth == 1) | (eighth == 3)
    a = jnp.where(swap, s, c)
    b = jnp.where(swap, c, s)
    a = jnp.where((eighth == 1) | (eighth == 2), -a, a)
    b = jnp.where((eighth == 2) | (eighth == 3), -b, b)
    return a, b


def features(chosen):
    amp = math.sqrt(2.0 / NACT)
    c0, s0 = cos_sin(chosen)
    cz, sz = cos_sin(wrap(chosen * stride_base))
    pc, ps = math.cos(phase_step), math.sin(phase_step)
    zr = cz * pc - sz * ps
    zi = cz * ps + sz * pc
    wr, wi = c0 * amp, s0 * amp
    out = [jnp.full(chosen.shape, 1.0 / math.sqrt(NACT), f32)]
    for _ in range(1, NACT):
        wr, wi = wr * zr - wi * zi, wr * zi + wi * zr
        out.append(wr)
    return out


def prepare(ctx_hbm, logged_hbm, policy_hbm, plane_ref, mine_ref, ctx_ref, logged_ref, policy_ref, sems):
    moves = [
        pltpu.make_async_copy(source, target, sems.at[i])
        for i, (source, target) in enumerate(
            ((ctx_hbm, ctx_ref), (logged_hbm, logged_ref), (policy_hbm, policy_ref))
        )
    ]
    for move in moves:
        move.start()
    for move in moves:
        move.wait()
    logged = jnp.concatenate(features(logged_ref[...]), axis=0)
    acts = policy_ref[...]
    codes = jnp.concatenate([acts >> 9, (acts & 511) - 256], axis=0).astype(f32)
    small = jnp.concatenate([logged, codes], axis=0).astype(bf16)
    ctx = ctx_ref[...]
    for i in range(PLANES):
        plane_ref[i, :TILE, :] = ctx
        plane_ref[i, TILE:, :] = small
    mine_ref[:TILE, :] = ctx
    mine_ref[TILE:, :] = small[:NACT]


def pieces(total):
    high = total.astype(bf16).astype(f32)
    rest = total - high
    middle = rest.astype(bf16).astype(f32)
    return high, middle, rest - middle


def lanes():
    return lax.broadcasted_iota(i32, (TILE, TILE), 1)


def policy_kernel(own_ref, other_ref, policy_ref, extra_ref):
    lane = lanes()
    for half, ref in enumerate((own_ref, other_ref)):
        for j in range(PLANES):
            at = 2 * j + half
            codes = ref[j, CODE_AT:ROWS, :].astype(f32).astype(i32)
            acts = (codes[:NPOL] << 9) + codes[NPOL:] + 256
            feats = jnp.concatenate(features(acts), axis=0).astype(bf16)
            policy_ref[:, at * TILE : (at + 1) * TILE] = feats
            wide = ref[j, :TILE, :].astype(f32)
            high, middle, low = pieces(jnp.sum(wide * wide, axis=1, keepdims=True))
            extra = jnp.where(lane == 0, high, jnp.where(lane == 1, middle, jnp.where(lane == 2, low, 1.0)))
            extra_ref[at] = extra.astype(bf16)


SCALE = math.log2(math.e) / D
CHUNK = 8
BESIDE = 1
NEAR = 2 + 2 * BESIDE
SPAN = 2 * CHUNK * TILE


def home(place_ref, at):
    upper, lower = place_ref[1] >> 2, place_ref[1] & 3
    return (((upper + at % 2) & 1) << 2) + ((lower + 4 - at // 2) & 3)


def pairs(own_ref, place_ref, partner_ref, moved):
    return [own_ref.at[place_ref[2]], partner_ref] + [ref.at[i] for ref in moved for i in range(2)]


def block(left_refs, right_refs, kernel_ref, acc, cols):
    own_ref, other_ref, policy_ref, extra_ref = left_refs
    lane = lanes()
    for b, right_ref in enumerate(right_refs):
        here = slice(b * TILE, (b + 1) * TILE)
        x = right_ref[:TILE, :].astype(f32)
        high, middle, low = pieces(jnp.sum(x * x, axis=1, keepdims=True))
        extra = jnp.where(lane < 3, -1.0, 0.0)
        for at, piece in ((3, high), (4, middle), (5, low)):
            extra = jnp.where(lane == at, -piece, extra)
        cols[here, :D] = (2.0 * x).astype(bf16)
        cols[here, D:] = extra.astype(bf16)
    width = len(right_refs) * TILE
    wide = 2 * TILE
    for step in range(PLANES // CHUNK):
        rows = jnp.concatenate(
            [
                jnp.concatenate([ref[j, :TILE, :], extra_ref[2 * j + half]], axis=1)
                for j in range(step * CHUNK, (step + 1) * CHUNK)
                for half, ref in enumerate((own_ref, other_ref))
            ],
            axis=0,
        )
        whole = slice(step * SPAN, (step + 1) * SPAN)
        for at in range(0, width, wide):
            span = slice(at, at + wide)
            expo = lax.dot_general(rows, cols[span, :], (((1,), (1,)), ((), ())), preferred_element_type=f32)
            kernel_ref[whole, span] = jnp.exp2(SCALE * expo).astype(bf16)
        term = jnp.dot(policy_ref[:, whole], kernel_ref[whole, :], preferred_element_type=f32)
        if step:
            term += acc[...]
        acc[...] = term
    sums = []
    for b, right_ref in enumerate(right_refs):
        chosen = right_ref[FEAT_AT : FEAT_AT + NACT, :].astype(f32)
        total = jnp.zeros((NPOL, TILE), f32)
        for c in range(NACT):
            total += acc[c * NPOL : (c + 1) * NPOL, b * TILE : (b + 1) * TILE] * chosen[c : c + 1]
        sums.append(total)
    return sums


def first_half(place_ref, own_ref, other_ref, policy_ref, extra_ref, *refs):
    right_refs = pairs(own_ref, place_ref, refs[0], refs[1 : 1 + BESIDE])
    kernel_ref, sums_ref, acc, cols = refs[1 + BESIDE :]
    for b, total in enumerate(block((own_ref, other_ref, policy_ref, extra_ref), right_refs, kernel_ref, acc, cols)):
        sums_ref[b] = total


def second_half(place_ref, own_ref, other_ref, policy_ref, extra_ref, done_ref, *refs):
    right_refs = [ref.at[i] for ref in refs[: 3 - BESIDE] for i in range(2)]
    kernel_ref, sums_ref, acc, cols = refs[3 - BESIDE :]
    totals = block((own_ref, other_ref, policy_ref, extra_ref), right_refs, kernel_ref, acc, cols)
    totals = [done_ref[b] for b in range(NEAR)] + totals
    for b, total in enumerate(totals):
        at = home(place_ref, b)
        for peer in range(COLUMNS):
            sums_ref[peer, at] = total


def second_kernel(place_ref, near_ref, far_ref, parts_ref, own_ref, other_ref, *refs):
    right_refs = pairs(own_ref, place_ref, refs[0], refs[1:4])
    image_ref, side_ref, matched = refs[4:]
    factor = NACT / (TILE * LEFT * COLUMNS)
    for b, right_ref in enumerate(right_refs):
        at = home(place_ref, b)
        total = parts_ref[0, at]
        for peer in range(1, COLUMNS):
            total += parts_ref[peer, at]
        total = total * factor
        if b == 0:
            side_ref[...] = total
        low = total.astype(bf16).astype(f32)
        chosen = right_ref[FEAT_AT : FEAT_AT + NACT, :].astype(f32)
        made = jnp.concatenate([chosen[c : c + 1] * low for c in range(NACT)], axis=0)
        matched[b * TILE : (b + 1) * TILE, :] = jnp.transpose(made).astype(bf16)
    core = place_ref[0]
    cut = NEAR * TILE
    for step in range(PLANES // CHUNK):
        whole = slice(step * SPAN, (step + 1) * SPAN)
        out = jnp.dot(near_ref[whole, :], matched[:cut, :], preferred_element_type=f32)
        out += jnp.dot(far_ref[whole, :], matched[cut:, :], preferred_element_type=f32)
        out = jnp.transpose(out)
        for j in range(step * CHUNK, (step + 1) * CHUNK):
            for half, ref in enumerate((own_ref, other_ref)):
                chosen = ref[j, FEAT_AT : FEAT_AT + NACT, :].astype(f32)
                at = (2 * (j - step * CHUNK) + half) * TILE
                total = jnp.zeros((NPOL, TILE), f32)
                for c in range(NACT):
                    total += out[c * NPOL : (c + 1) * NPOL, at : at + TILE] * chosen[c : c + 1]
                image_ref[2 * j + jnp.where(core == half, 0, 1)] = total * factor


def third_kernel(parts_ref, side_ref, rewards_ref, image_ref, sums_ref):
    total = parts_ref[0]
    for i in range(1, LEFT):
        total += parts_ref[i]
    side = side_ref[...]
    image = total + ridge * side
    image_ref[...] = image
    lane = lax.broadcasted_iota(i32, (NPOL, TILE), 1)
    row = lax.broadcasted_iota(i32, (NPOL, TILE), 0)
    spread = jnp.zeros((NPOL, TILE), f32)
    for k, value in enumerate((side * side, side * image, rewards_ref[...] * side)):
        spread = jnp.where(lane == row + k * NPOL, jnp.sum(value, axis=1, keepdims=True), spread)
    flat = jnp.sum(spread, axis=0, keepdims=True)
    sums_ref[...] = jnp.broadcast_to(flat, sums_ref.shape)


def last_kernel(sums_ref, image_ref, side_ref, weights_ref, residual_ref, values_ref):
    count = sums_ref.shape[0]
    total = jnp.sum(sums_ref[...], axis=0, keepdims=True)
    lane = lax.broadcasted_iota(i32, (NPOL, TILE), 1)
    row = lax.broadcasted_iota(i32, (NPOL, TILE), 0)
    wide = jnp.broadcast_to(total, (NPOL, TILE))

    def pick(k):
        return jnp.sum(jnp.where(lane == row + k * NPOL, wide, 0.0), axis=1, keepdims=True)

    alpha = pick(0) / pick(1)
    side = side_ref[...]
    weights_ref[...] = alpha * side
    residual_ref[...] = side - alpha * image_ref[...]
    values = alpha * pick(2) / (TILE * count)
    values_ref[...] = jnp.sum(jnp.where(lane == row, values, 0.0), axis=0, keepdims=True)[:, :NPOL]


def params(limit=32 * MIB):
    return pltpu.CompilerParams(vmem_limit_bytes=limit)


def exchange(value, axes):
    return lax.all_to_all(value, axes, 0, 0)


def on_device(contexts, logged_actions, policy_actions, rewards):
    core = lax.axis_index("core")
    column = lax.axis_index(COLUMN)
    place = jnp.stack([core, column, lax.axis_index(PLANE)]).astype(i32)
    sds = jax.ShapeDtypeStruct
    vmem = pl.BlockSpec(memory_space=pltpu.VMEM)
    smem = pl.BlockSpec(memory_space=pltpu.SMEM)

    plane_send, mine = pl.pallas_call(
        prepare,
        in_specs=[pl.BlockSpec(memory_space=pl.ANY)] * 3,
        out_shape=(sds((PLANES, ROWS, D), bf16), sds((RIGHT_ROWS, D), bf16)),
        scratch_shapes=[
            pltpu.VMEM((TILE, D), bf16),
            pltpu.VMEM((1, TILE), i32),
            pltpu.VMEM((NPOL, TILE), i32),
            pltpu.SemaphoreType.DMA((3,)),
        ],
        compiler_params=params(60 * MIB),
    )(contexts, logged_actions.reshape(1, TILE), policy_actions.T)
    partner = lax.ppermute(mine, "z_hi", [(0, 1), (1, 0)])
    pair = jnp.stack([mine, partner])
    moved = [lax.ppermute(pair, "z_lo", [(i, (i + shift) % 4) for i in range(4)]) for shift in range(1, 4)]
    own, partner, *moved[:BESIDE] = lax.optimization_barrier((exchange(plane_send, PLANE), partner, *moved[:BESIDE]))
    other = lax.ppermute(own, "core", [(0, 1), (1, 0)])

    policy, extra = pl.pallas_call(
        policy_kernel,
        out_shape=(sds((TILE, LEFT * TILE), bf16), sds((LEFT, TILE, TILE), bf16)),
        cost_estimate=pl.CostEstimate(flops=60_000_000, bytes_accessed=3_000_000, transcendentals=0),
        compiler_params=params(),
    )(own, other)
    left = (place, own, other, policy, extra)
    rows = LEFT * TILE

    def cost(width):
        return pl.CostEstimate(
            flops=2 * rows * width * (2 * D + TILE), bytes_accessed=2 * rows * (width + 4 * D), transcendentals=rows * width
        )

    near, far = NEAR * TILE, (COLUMNS - NEAR) * TILE
    scratch = lambda width: [pltpu.VMEM((TILE, width), f32), pltpu.VMEM((width, 2 * D), bf16)]
    near_block, done = pl.pallas_call(
        first_half,
        in_specs=[smem] + [vmem] * (5 + BESIDE),
        out_shape=(sds((rows, near), bf16), sds((NEAR, NPOL, TILE), f32)),
        scratch_shapes=scratch(near),
        cost_estimate=cost(near),
        compiler_params=params(),
    )(*left, partner, *moved[:BESIDE])
    far_block, first = pl.pallas_call(
        second_half,
        in_specs=[smem] + [vmem] * (8 - BESIDE),
        out_shape=(sds((rows, far), bf16), sds((COLUMNS, COLUMNS, NPOL, TILE), f32)),
        scratch_shapes=scratch(far),
        cost_estimate=cost(far),
        compiler_params=params(),
    )(*left, done, *moved[BESIDE:])
    parts = exchange(first, COLUMN)
    image_parts, side = pl.pallas_call(
        second_kernel,
        in_specs=[smem] + [vmem] * 9,
        out_shape=(sds((LEFT, NPOL, TILE), f32), sds((NPOL, TILE), f32)),
        scratch_shapes=[pltpu.VMEM((COLUMNS * TILE, TILE), bf16)],
        compiler_params=params(),
    )(place, near_block, far_block, parts, own, other, partner, *moved)
    image_parts = exchange(image_parts, PLANE + ("core",))

    count = LEFT * COLUMNS
    image, sums = pl.pallas_call(
        third_kernel,
                out_shape=(sds((NPOL, TILE), f32), sds((count, TILE), f32)),
        compiler_params=params(),
    )(image_parts, side, rewards.reshape(1, TILE))
    sums = exchange(sums.reshape(count, 1, TILE), EVERY).reshape(count, TILE)
    weights, residual, values = pl.pallas_call(
        last_kernel,
        out_shape=(sds((NPOL, TILE), f32), sds((NPOL, TILE), f32), sds((1, NPOL), f32)),
        compiler_params=params(),
    )(sums, image, side)
    return weights.T, residual.T, values.reshape(NPOL)


def solution(mesh):
    fine = Mesh(mesh.devices.reshape([size for _, size in SIZES]), EVERY)
    return jax.shard_map(
        on_device,
        mesh=fine,
        in_specs=(P(EVERY, None), P(EVERY), P(EVERY, None), P(EVERY)),
        out_specs=(P(EVERY, None), P(EVERY, None), P()),
        check_vma=False,
    )
```

```python
import math

import jax
import jax.numpy as jnp
from jax import lax
from jax.experimental import pallas as pl
from jax.experimental.pallas import tpu as pltpu
from jax.sharding import Mesh
from jax.sharding import PartitionSpec as P

NPOL = 8
NACT = 16
CATALOG = 131042
D = 128
TILE = 128

ridge = 0.1
stride_base = 1009
phase_step = 0.37
two_pi = 2.0 * math.pi

SIZES = (("z_hi", 2), ("x", 4), ("z_lo", 4), ("y", 4), ("core", 2))
EVERY = tuple(name for name, _ in SIZES)
PLANE = ("x", "y")
COLUMN = ("z_hi", "z_lo")
PLANES = 16
COLUMNS = 8
LEFT = 2 * PLANES
ROWS = 160
FEAT_AT, CODE_AT = 128, 144
RIGHT_ROWS = 144

f32, bf16, i32 = jnp.float32, jnp.bfloat16, jnp.int32
MIB = 1 << 20


def wrap(product):
    guess = (product.astype(f32) * (1.0 / CATALOG)).astype(i32)
    left = product - guess * CATALOG
    left = jnp.where(left < 0, left + CATALOG, left)
    return jnp.where(left >= CATALOG, left - CATALOG, left)


def cos_sin(turn):
    eighth = (turn.astype(f32) * (4.0 / CATALOG) + 0.5).astype(i32)
    rest = 4 * turn - eighth * CATALOG
    t = rest.astype(f32) * (two_pi / 4 / CATALOG)
    u = t * t
    s = t * (1.0 + u * (-1.0 / 6 + u * (1.0 / 120 + u * (-1.0 / 5040 + u * (1.0 / 362880)))))
    c = 1.0 + u * (-0.5 + u * (1.0 / 24 + u * (-1.0 / 720 + u * (1.0 / 40320))))
    swap = (eighth == 1) | (eighth == 3)
    a = jnp.where(swap, s, c)
    b = jnp.where(swap, c, s)
    a = jnp.where((eighth == 1) | (eighth == 2), -a, a)
    b = jnp.where((eighth == 2) | (eighth == 3), -b, b)
    return a, b


def features(chosen):
    amp = math.sqrt(2.0 / NACT)
    c0, s0 = cos_sin(chosen)
    cz, sz = cos_sin(wrap(chosen * stride_base))
    pc, ps = math.cos(phase_step), math.sin(phase_step)
    zr = cz * pc - sz * ps
    zi = cz * ps + sz * pc
    wr, wi = c0 * amp, s0 * amp
    out = [jnp.full(chosen.shape, 1.0 / math.sqrt(NACT), f32)]
    for _ in range(1, NACT):
        wr, wi = wr * zr - wi * zi, wr * zi + wi * zr
        out.append(wr)
    return out


def prepare(ctx_hbm, logged_hbm, policy_hbm, plane_ref, mine_ref, ctx_ref, logged_ref, policy_ref, sems):
    moves = [
        pltpu.make_async_copy(source, target, sems.at[i])
        for i, (source, target) in enumerate(
            ((ctx_hbm, ctx_ref), (logged_hbm, logged_ref), (policy_hbm, policy_ref))
        )
    ]
    for move in moves:
        move.start()
    for move in moves[1:]:
        move.wait()
    logged = jnp.concatenate(features(logged_ref[...]), axis=0)
    acts = policy_ref[...]
    codes = jnp.concatenate([acts >> 9, (acts & 511) - 256], axis=0).astype(f32)
    small = jnp.concatenate([logged, codes], axis=0).astype(bf16)
    moves[0].wait()
    ctx = ctx_ref[...]
    for i in range(PLANES):
        plane_ref[i, :TILE, :] = ctx
        plane_ref[i, TILE:, :] = small
    mine_ref[:TILE, :] = ctx
    mine_ref[TILE:, :] = small[:NACT]


def pieces(total):
    high = total.astype(bf16).astype(f32)
    rest = total - high
    middle = rest.astype(bf16).astype(f32)
    return high, middle, rest - middle


def lanes():
    return lax.broadcasted_iota(i32, (TILE, TILE), 1)


def policy_kernel(own_ref, other_ref, policy_ref, extra_ref):
    lane = lanes()
    for half, ref in enumerate((own_ref, other_ref)):
        for j in range(PLANES):
            at = 2 * j + half
            codes = ref[j, CODE_AT:ROWS, :].astype(f32).astype(i32)
            acts = (codes[:NPOL] << 9) + codes[NPOL:] + 256
            feats = jnp.concatenate(features(acts), axis=0).astype(bf16)
            policy_ref[:, at * TILE : (at + 1) * TILE] = feats
            wide = ref[j, :TILE, :].astype(f32)
            high, middle, low = pieces(jnp.sum(wide * wide, axis=1, keepdims=True))
            extra = jnp.where(lane == 0, high, jnp.where(lane == 1, middle, jnp.where(lane == 2, low, 1.0)))
            extra_ref[at] = extra.astype(bf16)


SCALE = math.log2(math.e) / D
CHUNK = 8
NEAR = 4
BESIDE = 4
SPAN = 2 * CHUNK * TILE


def home(place_ref, shift):
    return lax.rem(place_ref[1] + (COLUMNS - shift), COLUMNS)


def block(left_refs, right_refs, kernel_ref, acc, cols):
    own_ref, other_ref, policy_ref, extra_ref = left_refs
    lane = lanes()
    for b, right_ref in enumerate(right_refs):
        here = slice(b * TILE, (b + 1) * TILE)
        x = right_ref[:TILE, :].astype(f32)
        high, middle, low = pieces(jnp.sum(x * x, axis=1, keepdims=True))
        extra = jnp.where(lane < 3, -1.0, 0.0)
        for at, piece in ((3, high), (4, middle), (5, low)):
            extra = jnp.where(lane == at, -piece, extra)
        cols[here, :D] = (2.0 * x).astype(bf16)
        cols[here, D:] = extra.astype(bf16)
    width = len(right_refs) * TILE
    wide = 2 * TILE
    for step in range(PLANES // CHUNK):
        rows = jnp.concatenate(
            [
                jnp.concatenate([ref[j, :TILE, :], extra_ref[2 * j + half]], axis=1)
                for j in range(step * CHUNK, (step + 1) * CHUNK)
                for half, ref in enumerate((own_ref, other_ref))
            ],
            axis=0,
        )
        whole = slice(step * SPAN, (step + 1) * SPAN)
        for at in range(0, width, wide):
            span = slice(at, at + wide)
            expo = lax.dot_general(rows, cols[span, :], (((1,), (1,)), ((), ())), preferred_element_type=f32)
            kernel_ref[whole, span] = jnp.exp2(SCALE * expo).astype(bf16)
        term = jnp.dot(policy_ref[:, whole], kernel_ref[whole, :], preferred_element_type=f32)
        if step:
            term += acc[...]
        acc[...] = term
    sums = []
    for b, right_ref in enumerate(right_refs):
        chosen = right_ref[FEAT_AT : FEAT_AT + NACT, :].astype(f32)
        total = jnp.zeros((NPOL, TILE), f32)
        for c in range(NACT):
            total += acc[c * NPOL : (c + 1) * NPOL, b * TILE : (b + 1) * TILE] * chosen[c : c + 1]
        sums.append(total)
    return sums


def first_half(place_ref, own_ref, other_ref, policy_ref, extra_ref, *refs):
    right_refs = (own_ref.at[place_ref[2]], *refs[: NEAR - 1])
    kernel_ref, sums_ref, acc, cols = refs[NEAR - 1 :]
    for b, total in enumerate(block((own_ref, other_ref, policy_ref, extra_ref), right_refs, kernel_ref, acc, cols)):
        sums_ref[b] = total


def second_half(place_ref, own_ref, other_ref, policy_ref, extra_ref, done_ref, *refs):
    right_refs = refs[: COLUMNS - NEAR]
    kernel_ref, sums_ref, acc, cols = refs[COLUMNS - NEAR :]
    totals = block((own_ref, other_ref, policy_ref, extra_ref), right_refs, kernel_ref, acc, cols)
    totals = [done_ref[b] for b in range(NEAR)] + totals
    for b, total in enumerate(totals):
        at = home(place_ref, b)
        for peer in range(COLUMNS):
            sums_ref[peer, at] = total


def second_kernel(place_ref, near_ref, far_ref, parts_ref, own_ref, other_ref, *refs):
    right_refs = (own_ref.at[place_ref[2]], *refs[: COLUMNS - 1])
    image_ref, side_ref, matched = refs[COLUMNS - 1 :]
    factor = NACT / (TILE * LEFT * COLUMNS)
    for b, right_ref in enumerate(right_refs):
        at = home(place_ref, b)
        total = parts_ref[0, at]
        for peer in range(1, COLUMNS):
            total += parts_ref[peer, at]
        total = total * factor
        if b == 0:
            side_ref[...] = total
        low = total.astype(bf16).astype(f32)
        chosen = right_ref[FEAT_AT : FEAT_AT + NACT, :].astype(f32)
        made = jnp.concatenate([chosen[c : c + 1] * low for c in range(NACT)], axis=0)
        matched[b * TILE : (b + 1) * TILE, :] = jnp.transpose(made).astype(bf16)
    core = place_ref[0]
    cut = NEAR * TILE
    for step in range(PLANES // CHUNK):
        whole = slice(step * SPAN, (step + 1) * SPAN)
        out = jnp.dot(near_ref[whole, :], matched[:cut, :], preferred_element_type=f32)
        out += jnp.dot(far_ref[whole, :], matched[cut:, :], preferred_element_type=f32)
        out = jnp.transpose(out)
        for j in range(step * CHUNK, (step + 1) * CHUNK):
            for half, ref in enumerate((own_ref, other_ref)):
                chosen = ref[j, FEAT_AT : FEAT_AT + NACT, :].astype(f32)
                at = (2 * (j - step * CHUNK) + half) * TILE
                total = jnp.zeros((NPOL, TILE), f32)
                for c in range(NACT):
                    total += out[c * NPOL : (c + 1) * NPOL, at : at + TILE] * chosen[c : c + 1]
                image_ref[2 * j + jnp.where(core == half, 0, 1)] = total * factor


def third_kernel(parts_ref, side_ref, rewards_ref, image_ref, sums_ref):
    total = parts_ref[0]
    for i in range(1, LEFT):
        total += parts_ref[i]
    side = side_ref[...]
    image = total + ridge * side
    image_ref[...] = image
    lane = lax.broadcasted_iota(i32, (NPOL, TILE), 1)
    row = lax.broadcasted_iota(i32, (NPOL, TILE), 0)
    spread = jnp.zeros((NPOL, TILE), f32)
    for k, value in enumerate((side * side, side * image, rewards_ref[...] * side)):
        spread = jnp.where(lane == row + k * NPOL, jnp.sum(value, axis=1, keepdims=True), spread)
    flat = jnp.sum(spread, axis=0, keepdims=True)
    sums_ref[...] = jnp.broadcast_to(flat, sums_ref.shape)


def last_kernel(sums_ref, image_ref, side_ref, weights_ref, residual_ref, values_ref):
    count = sums_ref.shape[0]
    total = jnp.sum(sums_ref[...], axis=0, keepdims=True)
    lane = lax.broadcasted_iota(i32, (NPOL, TILE), 1)
    row = lax.broadcasted_iota(i32, (NPOL, TILE), 0)
    wide = jnp.broadcast_to(total, (NPOL, TILE))

    def pick(k):
        return jnp.sum(jnp.where(lane == row + k * NPOL, wide, 0.0), axis=1, keepdims=True)

    alpha = pick(0) / pick(1)
    side = side_ref[...]
    weights_ref[...] = alpha * side
    residual_ref[...] = side - alpha * image_ref[...]
    values = alpha * pick(2) / (TILE * count)
    values_ref[...] = jnp.sum(jnp.where(lane == row, values, 0.0), axis=0, keepdims=True)[:, :NPOL]


def params(limit=32 * MIB):
    return pltpu.CompilerParams(vmem_limit_bytes=limit)


def exchange(value, axes):
    return lax.all_to_all(value, axes, 0, 0)


def on_device(contexts, logged_actions, policy_actions, rewards):
    core = lax.axis_index("core")
    column = lax.axis_index(COLUMN)
    place = jnp.stack([core, column, lax.axis_index(PLANE)]).astype(i32)
    sds = jax.ShapeDtypeStruct
    vmem = pl.BlockSpec(memory_space=pltpu.VMEM)
    smem = pl.BlockSpec(memory_space=pltpu.SMEM)

    plane_send, mine = pl.pallas_call(
        prepare,
        in_specs=[pl.BlockSpec(memory_space=pl.ANY)] * 3,
        out_shape=(sds((PLANES, ROWS, D), bf16), sds((RIGHT_ROWS, D), bf16)),
        scratch_shapes=[
            pltpu.VMEM((TILE, D), bf16),
            pltpu.VMEM((1, TILE), i32),
            pltpu.VMEM((NPOL, TILE), i32),
            pltpu.SemaphoreType.DMA((3,)),
        ],
        compiler_params=params(60 * MIB),
    )(contexts, logged_actions.reshape(1, TILE), policy_actions.T)
    ring = lambda shift: [(i, (i + shift) % COLUMNS) for i in range(COLUMNS)]
    right = [lax.ppermute(mine, COLUMN, ring(shift)) for shift in range(1, COLUMNS)]
    own, *right[:BESIDE] = lax.optimization_barrier((exchange(plane_send, PLANE), *right[:BESIDE]))
    other = lax.ppermute(own, "core", [(0, 1), (1, 0)])

    policy, extra = pl.pallas_call(
        policy_kernel,
        out_shape=(sds((TILE, LEFT * TILE), bf16), sds((LEFT, TILE, TILE), bf16)),
        cost_estimate=pl.CostEstimate(flops=60_000_000, bytes_accessed=3_000_000, transcendentals=0),
        compiler_params=params(),
    )(own, other)
    left = (place, own, other, policy, extra)
    rows = LEFT * TILE

    def cost(width):
        return pl.CostEstimate(
            flops=2 * rows * width * (2 * D + TILE), bytes_accessed=2 * rows * (width + 4 * D), transcendentals=rows * width
        )

    near, far = NEAR * TILE, (COLUMNS - NEAR) * TILE
    scratch = lambda width: [pltpu.VMEM((TILE, width), f32), pltpu.VMEM((width, 2 * D), bf16)]
    near_block, done = pl.pallas_call(
        first_half,
        in_specs=[smem] + [vmem] * (3 + NEAR),
        out_shape=(sds((rows, near), bf16), sds((NEAR, NPOL, TILE), f32)),
        scratch_shapes=scratch(near),
        cost_estimate=cost(near),
        compiler_params=params(),
    )(*left, *right[: NEAR - 1])
    far_block, first = pl.pallas_call(
        second_half,
        in_specs=[smem] + [vmem] * (5 + COLUMNS - NEAR),
        out_shape=(sds((rows, far), bf16), sds((COLUMNS, COLUMNS, NPOL, TILE), f32)),
        scratch_shapes=scratch(far),
        cost_estimate=cost(far),
        compiler_params=params(),
    )(*left, done, *right[NEAR - 1 :])
    parts = exchange(first, COLUMN)
    image_parts, side = pl.pallas_call(
        second_kernel,
        in_specs=[smem] + [vmem] * (4 + COLUMNS),
        out_shape=(sds((LEFT, NPOL, TILE), f32), sds((NPOL, TILE), f32)),
        scratch_shapes=[pltpu.VMEM((COLUMNS * TILE, TILE), bf16)],
        compiler_params=params(),
    )(place, near_block, far_block, parts, own, other, *right)
    image_parts = exchange(image_parts, PLANE + ("core",))

    count = LEFT * COLUMNS
    image, sums = pl.pallas_call(
        third_kernel,
                out_shape=(sds((NPOL, TILE), f32), sds((count, TILE), f32)),
        compiler_params=params(),
    )(image_parts, side, rewards.reshape(1, TILE))
    sums = exchange(sums.reshape(count, 1, TILE), EVERY).reshape(count, TILE)
    weights, residual, values = pl.pallas_call(
        last_kernel,
        out_shape=(sds((NPOL, TILE), f32), sds((NPOL, TILE), f32), sds((1, NPOL), f32)),
        compiler_params=params(),
    )(sums, image, side)
    return weights.T, residual.T, values.reshape(NPOL)


def solution(mesh):
    fine = Mesh(mesh.devices.reshape([size for _, size in SIZES]), EVERY)
    return jax.shard_map(
        on_device,
        mesh=fine,
        in_specs=(P(EVERY, None), P(EVERY), P(EVERY, None), P(EVERY)),
        out_specs=(P(EVERY, None), P(EVERY, None), P()),
        check_vma=False,
    )
```

```python
import math

import jax
import jax.numpy as jnp
from jax import lax
from jax.experimental import pallas as pl
from jax.experimental.pallas import tpu as pltpu
from jax.sharding import Mesh
from jax.sharding import PartitionSpec as P

NPOL = 8
NACT = 16
CATALOG = 131042
D = 128
TILE = 128

ridge = 0.1
stride_base = 1009
phase_step = 0.37
two_pi = 2.0 * math.pi

SIZES = (("z_hi", 2), ("x", 4), ("z_lo", 4), ("y", 4), ("core", 2))
EVERY = tuple(name for name, _ in SIZES)
PLANE = ("x", "y")
COLUMN = ("z_hi", "z_lo")
PLANES = 16
COLUMNS = 8
LEFT = 2 * PLANES
ROWS = 160
FEAT_AT, CODE_AT = 128, 144
RIGHT_ROWS = 144

f32, bf16, i32 = jnp.float32, jnp.bfloat16, jnp.int32
MIB = 1 << 20


def wrap(product):
    guess = (product.astype(f32) * (1.0 / CATALOG)).astype(i32)
    left = product - guess * CATALOG
    left = jnp.where(left < 0, left + CATALOG, left)
    return jnp.where(left >= CATALOG, left - CATALOG, left)


def cos_sin(turn):
    eighth = (turn.astype(f32) * (4.0 / CATALOG) + 0.5).astype(i32)
    rest = 4 * turn - eighth * CATALOG
    t = rest.astype(f32) * (two_pi / 4 / CATALOG)
    u = t * t
    s = t * (1.0 + u * (-1.0 / 6 + u * (1.0 / 120 + u * (-1.0 / 5040 + u * (1.0 / 362880)))))
    c = 1.0 + u * (-0.5 + u * (1.0 / 24 + u * (-1.0 / 720 + u * (1.0 / 40320))))
    swap = (eighth == 1) | (eighth == 3)
    a = jnp.where(swap, s, c)
    b = jnp.where(swap, c, s)
    a = jnp.where((eighth == 1) | (eighth == 2), -a, a)
    b = jnp.where((eighth == 2) | (eighth == 3), -b, b)
    return a, b


def features(chosen):
    amp = math.sqrt(2.0 / NACT)
    c0, s0 = cos_sin(chosen)
    cz, sz = cos_sin(wrap(chosen * stride_base))
    pc, ps = math.cos(phase_step), math.sin(phase_step)
    zr = cz * pc - sz * ps
    zi = cz * ps + sz * pc
    wr, wi = c0 * amp, s0 * amp
    out = [jnp.full(chosen.shape, 1.0 / math.sqrt(NACT), f32)]
    for _ in range(1, NACT):
        wr, wi = wr * zr - wi * zi, wr * zi + wi * zr
        out.append(wr)
    return out


def prepare(ctx_hbm, logged_hbm, policy_hbm, plane_ref, mine_ref, ctx_ref, logged_ref, policy_ref, sems):
    moves = [
        pltpu.make_async_copy(source, target, sems.at[i])
        for i, (source, target) in enumerate(
            ((ctx_hbm, ctx_ref), (logged_hbm, logged_ref), (policy_hbm, policy_ref))
        )
    ]
    for move in moves:
        move.start()
    for move in moves[1:]:
        move.wait()
    logged = jnp.concatenate(features(logged_ref[...]), axis=0)
    acts = policy_ref[...]
    codes = jnp.concatenate([acts >> 9, (acts & 511) - 256], axis=0).astype(f32)
    small = jnp.concatenate([logged, codes], axis=0).astype(bf16)
    moves[0].wait()
    ctx = ctx_ref[...]
    for i in range(PLANES):
        plane_ref[i, :TILE, :] = ctx
        plane_ref[i, TILE:, :] = small
    mine_ref[:TILE, :] = ctx
    mine_ref[TILE:, :] = small[:NACT]


def pieces(total):
    high = total.astype(bf16).astype(f32)
    rest = total - high
    middle = rest.astype(bf16).astype(f32)
    return high, middle, rest - middle


def lanes():
    return lax.broadcasted_iota(i32, (TILE, TILE), 1)


def policy_kernel(own_ref, other_ref, policy_ref, extra_ref):
    lane = lanes()
    for half, ref in enumerate((own_ref, other_ref)):
        for j in range(PLANES):
            at = 2 * j + half
            codes = ref[j, CODE_AT:ROWS, :].astype(f32).astype(i32)
            acts = (codes[:NPOL] << 9) + codes[NPOL:] + 256
            feats = jnp.concatenate(features(acts), axis=0).astype(bf16)
            policy_ref[:, at * TILE : (at + 1) * TILE] = feats
            wide = ref[j, :TILE, :].astype(f32)
            high, middle, low = pieces(jnp.sum(wide * wide, axis=1, keepdims=True))
            extra = jnp.where(lane == 0, high, jnp.where(lane == 1, middle, jnp.where(lane == 2, low, 1.0)))
            extra_ref[at] = extra.astype(bf16)


SCALE = math.log2(math.e) / D
CHUNK = 8
NEAR = 4
BESIDE = 4
SPAN = 2 * CHUNK * TILE


def home(place_ref, shift):
    return lax.rem(place_ref[1] + (COLUMNS - shift), COLUMNS)


def block(left_refs, right_refs, kernel_ref, acc, cols):
    own_ref, other_ref, policy_ref, extra_ref = left_refs
    lane = lanes()
    for b, right_ref in enumerate(right_refs):
        here = slice(b * TILE, (b + 1) * TILE)
        x = right_ref[:TILE, :].astype(f32)
        high, middle, low = pieces(jnp.sum(x * x, axis=1, keepdims=True))
        extra = jnp.where(lane < 3, -1.0, 0.0)
        for at, piece in ((3, high), (4, middle), (5, low)):
            extra = jnp.where(lane == at, -piece, extra)
        cols[here, :D] = (2.0 * x).astype(bf16)
        cols[here, D:] = extra.astype(bf16)
    width = len(right_refs) * TILE
    wide = 2 * TILE
    for step in range(PLANES // CHUNK):
        rows = jnp.concatenate(
            [
                jnp.concatenate([ref[j, :TILE, :], extra_ref[2 * j + half]], axis=1)
                for j in range(step * CHUNK, (step + 1) * CHUNK)
                for half, ref in enumerate((own_ref, other_ref))
            ],
            axis=0,
        )
        whole = slice(step * SPAN, (step + 1) * SPAN)
        for at in range(0, width, wide):
            span = slice(at, at + wide)
            expo = lax.dot_general(rows, cols[span, :], (((1,), (1,)), ((), ())), preferred_element_type=f32)
            kernel_ref[whole, span] = jnp.exp2(SCALE * expo).astype(bf16)
        term = jnp.dot(policy_ref[:, whole], kernel_ref[whole, :], preferred_element_type=f32)
        if step:
            term += acc[...]
        acc[...] = term
    sums = []
    for b, right_ref in enumerate(right_refs):
        chosen = right_ref[FEAT_AT : FEAT_AT + NACT, :].astype(f32)
        total = jnp.zeros((NPOL, TILE), f32)
        for c in range(NACT):
            total += acc[c * NPOL : (c + 1) * NPOL, b * TILE : (b + 1) * TILE] * chosen[c : c + 1]
        sums.append(total)
    return sums


def first_half(place_ref, own_ref, other_ref, policy_ref, extra_ref, *refs):
    right_refs = (own_ref.at[place_ref[2]], *refs[: NEAR - 1])
    kernel_ref, sums_ref, acc, cols = refs[NEAR - 1 :]
    for b, total in enumerate(block((own_ref, other_ref, policy_ref, extra_ref), right_refs, kernel_ref, acc, cols)):
        sums_ref[b] = total


def second_half(place_ref, own_ref, other_ref, policy_ref, extra_ref, done_ref, *refs):
    right_refs = refs[: COLUMNS - NEAR]
    kernel_ref, sums_ref, acc, cols = refs[COLUMNS - NEAR :]
    totals = block((own_ref, other_ref, policy_ref, extra_ref), right_refs, kernel_ref, acc, cols)
    totals = [done_ref[b] for b in range(NEAR)] + totals
    for b, total in enumerate(totals):
        at = home(place_ref, b)
        high, middle, low = (piece.astype(bf16) for piece in pieces(total))
        for peer in range(COLUMNS):
            sums_ref[peer, at] = high
        sums_ref[at, COLUMNS] = middle
        sums_ref[at, COLUMNS + 1] = low


def second_kernel(place_ref, near_ref, far_ref, parts_ref, own_ref, other_ref, *refs):
    right_refs = (own_ref.at[place_ref[2]], *refs[: COLUMNS - 1])
    image_ref, side_ref, matched = refs[COLUMNS - 1 :]
    factor = NACT / (TILE * LEFT * COLUMNS)
    for b, right_ref in enumerate(right_refs):
        at = home(place_ref, b)
        total = jnp.zeros((NPOL, TILE), f32)
        for peer in range(COLUMNS):
            part = parts_ref[peer, at].astype(f32)
            if b == 0:
                part += parts_ref[peer, COLUMNS].astype(f32)
                part += parts_ref[peer, COLUMNS + 1].astype(f32)
            total += part
        total = total * factor
        if b == 0:
            side_ref[...] = total
        low = total.astype(bf16).astype(f32)
        chosen = right_ref[FEAT_AT : FEAT_AT + NACT, :].astype(f32)
        made = jnp.concatenate([chosen[c : c + 1] * low for c in range(NACT)], axis=0)
        matched[b * TILE : (b + 1) * TILE, :] = jnp.transpose(made).astype(bf16)
    core = place_ref[0]
    cut = NEAR * TILE
    for step in range(PLANES // CHUNK):
        whole = slice(step * SPAN, (step + 1) * SPAN)
        out = jnp.dot(near_ref[whole, :], matched[:cut, :], preferred_element_type=f32)
        out += jnp.dot(far_ref[whole, :], matched[cut:, :], preferred_element_type=f32)
        out = jnp.transpose(out)
        for j in range(step * CHUNK, (step + 1) * CHUNK):
            for half, ref in enumerate((own_ref, other_ref)):
                chosen = ref[j, FEAT_AT : FEAT_AT + NACT, :].astype(f32)
                at = (2 * (j - step * CHUNK) + half) * TILE
                total = jnp.zeros((NPOL, TILE), f32)
                for c in range(NACT):
                    total += out[c * NPOL : (c + 1) * NPOL, at : at + TILE] * chosen[c : c + 1]
                image_ref[2 * j + jnp.where(core == half, 0, 1)] = total * factor


def third_kernel(parts_ref, side_ref, rewards_ref, image_ref, sums_ref):
    total = parts_ref[0]
    for i in range(1, LEFT):
        total += parts_ref[i]
    side = side_ref[...]
    image = total + ridge * side
    image_ref[...] = image
    lane = lax.broadcasted_iota(i32, (NPOL, TILE), 1)
    row = lax.broadcasted_iota(i32, (NPOL, TILE), 0)
    spread = jnp.zeros((NPOL, TILE), f32)
    for k, value in enumerate((side * side, side * image, rewards_ref[...] * side)):
        spread = jnp.where(lane == row + k * NPOL, jnp.sum(value, axis=1, keepdims=True), spread)
    flat = jnp.sum(spread, axis=0, keepdims=True)
    sums_ref[...] = jnp.broadcast_to(flat, sums_ref.shape)


def last_kernel(sums_ref, image_ref, side_ref, weights_ref, residual_ref, values_ref):
    count = sums_ref.shape[0]
    total = jnp.sum(sums_ref[...], axis=0, keepdims=True)
    lane = lax.broadcasted_iota(i32, (NPOL, TILE), 1)
    row = lax.broadcasted_iota(i32, (NPOL, TILE), 0)
    wide = jnp.broadcast_to(total, (NPOL, TILE))

    def pick(k):
        return jnp.sum(jnp.where(lane == row + k * NPOL, wide, 0.0), axis=1, keepdims=True)

    alpha = pick(0) / pick(1)
    side = side_ref[...]
    weights_ref[...] = alpha * side
    residual_ref[...] = side - alpha * image_ref[...]
    values = alpha * pick(2) / (TILE * count)
    values_ref[...] = jnp.sum(jnp.where(lane == row, values, 0.0), axis=0, keepdims=True)[:, :NPOL]


def params(limit=32 * MIB):
    return pltpu.CompilerParams(vmem_limit_bytes=limit)


def exchange(value, axes):
    return lax.all_to_all(value, axes, 0, 0)


def on_device(contexts, logged_actions, policy_actions, rewards):
    core = lax.axis_index("core")
    column = lax.axis_index(COLUMN)
    place = jnp.stack([core, column, lax.axis_index(PLANE)]).astype(i32)
    sds = jax.ShapeDtypeStruct
    vmem = pl.BlockSpec(memory_space=pltpu.VMEM)
    smem = pl.BlockSpec(memory_space=pltpu.SMEM)

    plane_send, mine = pl.pallas_call(
        prepare,
        in_specs=[pl.BlockSpec(memory_space=pl.ANY)] * 3,
        out_shape=(sds((PLANES, ROWS, D), bf16), sds((RIGHT_ROWS, D), bf16)),
        scratch_shapes=[
            pltpu.VMEM((TILE, D), bf16),
            pltpu.VMEM((1, TILE), i32),
            pltpu.VMEM((NPOL, TILE), i32),
            pltpu.SemaphoreType.DMA((3,)),
        ],
        compiler_params=params(60 * MIB),
    )(contexts, logged_actions.reshape(1, TILE), policy_actions.T)
    ring = lambda shift: [(i, (i + shift) % COLUMNS) for i in range(COLUMNS)]
    right = [lax.ppermute(mine, COLUMN, ring(shift)) for shift in range(1, COLUMNS)]
    own, *right[:BESIDE] = lax.optimization_barrier((exchange(plane_send, PLANE), *right[:BESIDE]))
    other = lax.ppermute(own, "core", [(0, 1), (1, 0)])

    policy, extra = pl.pallas_call(
        policy_kernel,
        out_shape=(sds((TILE, LEFT * TILE), bf16), sds((LEFT, TILE, TILE), bf16)),
        cost_estimate=pl.CostEstimate(flops=60_000_000, bytes_accessed=3_000_000, transcendentals=0),
        compiler_params=params(),
    )(own, other)
    left = (place, own, other, policy, extra)
    rows = LEFT * TILE

    def cost(width):
        return pl.CostEstimate(
            flops=2 * rows * width * (2 * D + TILE), bytes_accessed=2 * rows * (width + 4 * D), transcendentals=rows * width
        )

    near, far = NEAR * TILE, (COLUMNS - NEAR) * TILE
    scratch = lambda width: [pltpu.VMEM((TILE, width), f32), pltpu.VMEM((width, 2 * D), bf16)]
    near_block, done = pl.pallas_call(
        first_half,
        in_specs=[smem] + [vmem] * (3 + NEAR),
        out_shape=(sds((rows, near), bf16), sds((NEAR, NPOL, TILE), f32)),
        scratch_shapes=scratch(near),
        cost_estimate=cost(near),
        compiler_params=params(),
    )(*left, *right[: NEAR - 1])
    far_block, first = pl.pallas_call(
        second_half,
        in_specs=[smem] + [vmem] * (5 + COLUMNS - NEAR),
        out_shape=(sds((rows, far), bf16), sds((COLUMNS, COLUMNS + 2, NPOL, TILE), bf16)),
        scratch_shapes=scratch(far),
        cost_estimate=cost(far),
        compiler_params=params(),
    )(*left, done, *right[NEAR - 1 :])
    parts = exchange(first, COLUMN)
    image_parts, side = pl.pallas_call(
        second_kernel,
        in_specs=[smem] + [vmem] * (4 + COLUMNS),
        out_shape=(sds((LEFT, NPOL, TILE), f32), sds((NPOL, TILE), f32)),
        scratch_shapes=[pltpu.VMEM((COLUMNS * TILE, TILE), bf16)],
        compiler_params=params(),
    )(place, near_block, far_block, parts, own, other, *right)
    image_parts = exchange(image_parts, PLANE + ("core",))

    count = LEFT * COLUMNS
    image, sums = pl.pallas_call(
        third_kernel,
                out_shape=(sds((NPOL, TILE), f32), sds((count, TILE), f32)),
        compiler_params=params(),
    )(image_parts, side, rewards.reshape(1, TILE))
    sums = exchange(sums.reshape(count, 1, TILE), EVERY).reshape(count, TILE)
    weights, residual, values = pl.pallas_call(
        last_kernel,
        out_shape=(sds((NPOL, TILE), f32), sds((NPOL, TILE), f32), sds((1, NPOL), f32)),
        compiler_params=params(),
    )(sums, image, side)
    return weights.T, residual.T, values.reshape(NPOL)


def solution(mesh):
    fine = Mesh(mesh.devices.reshape([size for _, size in SIZES]), EVERY)
    return jax.shard_map(
        on_device,
        mesh=fine,
        in_specs=(P(EVERY, None), P(EVERY), P(EVERY, None), P(EVERY)),
        out_specs=(P(EVERY, None), P(EVERY, None), P()),
        check_vma=False,
    )
```

```python
import math

import jax
import jax.numpy as jnp
from jax import lax
from jax.experimental import pallas as pl
from jax.experimental.pallas import tpu as pltpu
from jax.sharding import Mesh
from jax.sharding import PartitionSpec as P

NPOL = 8
NACT = 16
CATALOG = 131042
D = 128
TILE = 128

ridge = 0.1
stride_base = 1009
phase_step = 0.37
two_pi = 2.0 * math.pi

SIZES = (("z_hi", 2), ("x", 4), ("z_lo", 4), ("y", 4), ("core", 2))
EVERY = tuple(name for name, _ in SIZES)
PLANE = ("x", "y")
COLUMN = ("z_hi", "z_lo")
PLANES = 16
COLUMNS = 8
LEFT = 2 * PLANES
ROWS = 160
FEAT_AT, CODE_AT = 128, 144
RIGHT_ROWS = 144

f32, bf16, i32 = jnp.float32, jnp.bfloat16, jnp.int32
MIB = 1 << 20


def wrap(product):
    guess = (product.astype(f32) * (1.0 / CATALOG)).astype(i32)
    left = product - guess * CATALOG
    left = jnp.where(left < 0, left + CATALOG, left)
    return jnp.where(left >= CATALOG, left - CATALOG, left)


def cos_sin(turn):
    eighth = (turn.astype(f32) * (4.0 / CATALOG) + 0.5).astype(i32)
    rest = 4 * turn - eighth * CATALOG
    t = rest.astype(f32) * (two_pi / 4 / CATALOG)
    u = t * t
    s = t * (1.0 + u * (-1.0 / 6 + u * (1.0 / 120 + u * (-1.0 / 5040 + u * (1.0 / 362880)))))
    c = 1.0 + u * (-0.5 + u * (1.0 / 24 + u * (-1.0 / 720 + u * (1.0 / 40320))))
    swap = (eighth == 1) | (eighth == 3)
    a = jnp.where(swap, s, c)
    b = jnp.where(swap, c, s)
    a = jnp.where((eighth == 1) | (eighth == 2), -a, a)
    b = jnp.where((eighth == 2) | (eighth == 3), -b, b)
    return a, b


def features(chosen):
    amp = math.sqrt(2.0 / NACT)
    c0, s0 = cos_sin(chosen)
    cz, sz = cos_sin(wrap(chosen * stride_base))
    pc, ps = math.cos(phase_step), math.sin(phase_step)
    zr = cz * pc - sz * ps
    zi = cz * ps + sz * pc
    wr, wi = c0 * amp, s0 * amp
    out = [jnp.full(chosen.shape, 1.0 / math.sqrt(NACT), f32)]
    for _ in range(1, NACT):
        wr, wi = wr * zr - wi * zi, wr * zi + wi * zr
        out.append(wr)
    return out


def prepare(ctx_hbm, logged_hbm, policy_hbm, plane_ref, mine_ref, ctx_ref, logged_ref, policy_ref, sems):
    moves = [
        pltpu.make_async_copy(source, target, sems.at[i])
        for i, (source, target) in enumerate(
            ((ctx_hbm, ctx_ref), (logged_hbm, logged_ref), (policy_hbm, policy_ref))
        )
    ]
    for move in moves:
        move.start()
    for move in moves[1:]:
        move.wait()
    logged = jnp.concatenate(features(logged_ref[...]), axis=0)
    acts = policy_ref[...]
    codes = jnp.concatenate([acts >> 9, (acts & 511) - 256], axis=0).astype(f32)
    small = jnp.concatenate([logged, codes], axis=0).astype(bf16)
    moves[0].wait()
    ctx = ctx_ref[...]
    for i in range(PLANES):
        plane_ref[i, :TILE, :] = ctx
        plane_ref[i, TILE:, :] = small
    mine_ref[:TILE, :] = ctx
    mine_ref[TILE:, :] = small[:NACT]


def pieces(total):
    high = total.astype(bf16).astype(f32)
    rest = total - high
    middle = rest.astype(bf16).astype(f32)
    return high, middle, rest - middle


def lanes():
    return lax.broadcasted_iota(i32, (TILE, TILE), 1)


def policy_kernel(own_ref, other_ref, policy_ref, extra_ref):
    lane = lanes()
    for half, ref in enumerate((own_ref, other_ref)):
        for j in range(PLANES):
            at = 2 * j + half
            codes = ref[j, CODE_AT:ROWS, :].astype(f32).astype(i32)
            acts = (codes[:NPOL] << 9) + codes[NPOL:] + 256
            feats = jnp.concatenate(features(acts), axis=0).astype(bf16)
            policy_ref[:, at * TILE : (at + 1) * TILE] = feats
            wide = ref[j, :TILE, :].astype(f32)
            high, middle, low = pieces(jnp.sum(wide * wide, axis=1, keepdims=True))
            extra = jnp.where(lane == 0, high, jnp.where(lane == 1, middle, jnp.where(lane == 2, low, 1.0)))
            extra_ref[at] = extra.astype(bf16)


SCALE = math.log2(math.e) / D
CHUNK = 4
NEAR = 4
BESIDE = 4
SPAN = 2 * CHUNK * TILE


def home(place_ref, shift):
    return lax.rem(place_ref[1] + (COLUMNS - shift), COLUMNS)


def block(left_refs, right_refs, kernel_ref, acc, cols):
    own_ref, other_ref, policy_ref, extra_ref = left_refs
    lane = lanes()
    for b, right_ref in enumerate(right_refs):
        here = slice(b * TILE, (b + 1) * TILE)
        x = right_ref[:TILE, :].astype(f32)
        high, middle, low = pieces(jnp.sum(x * x, axis=1, keepdims=True))
        extra = jnp.where(lane < 3, -1.0, 0.0)
        for at, piece in ((3, high), (4, middle), (5, low)):
            extra = jnp.where(lane == at, -piece, extra)
        cols[here, :D] = (2.0 * x).astype(bf16)
        cols[here, D:] = extra.astype(bf16)
    for step in range(PLANES // CHUNK):
        for j in range(step * CHUNK, (step + 1) * CHUNK):
            rows = jnp.concatenate(
                [
                    jnp.concatenate([ref[j, :TILE, :], extra_ref[2 * j + half]], axis=1)
                    for half, ref in enumerate((own_ref, other_ref))
                ],
                axis=0,
            )
            expo = lax.dot_general(cols[...], rows, (((1,), (1,)), ((), ())), preferred_element_type=f32)
            kernel_ref[:, 2 * j * TILE : 2 * (j + 1) * TILE] = jnp.exp2(SCALE * expo).astype(bf16)
        whole = slice(step * SPAN, (step + 1) * SPAN)
        term = lax.dot_general(
            policy_ref[:, whole], kernel_ref[:, whole], (((1,), (1,)), ((), ())), preferred_element_type=f32
        )
        if step:
            term += acc[...]
        acc[...] = term
    sums = []
    for b, right_ref in enumerate(right_refs):
        chosen = right_ref[FEAT_AT : FEAT_AT + NACT, :].astype(f32)
        total = jnp.zeros((NPOL, TILE), f32)
        for c in range(NACT):
            total += acc[c * NPOL : (c + 1) * NPOL, b * TILE : (b + 1) * TILE] * chosen[c : c + 1]
        sums.append(total)
    return sums


def first_half(place_ref, own_ref, other_ref, policy_ref, extra_ref, *refs):
    right_refs = (own_ref.at[place_ref[2]], *refs[: NEAR - 1])
    kernel_ref, sums_ref, acc, cols = refs[NEAR - 1 :]
    for b, total in enumerate(block((own_ref, other_ref, policy_ref, extra_ref), right_refs, kernel_ref, acc, cols)):
        sums_ref[b] = total


def second_half(place_ref, own_ref, other_ref, policy_ref, extra_ref, done_ref, *refs):
    right_refs = refs[: COLUMNS - NEAR]
    kernel_ref, sums_ref, acc, cols = refs[COLUMNS - NEAR :]
    totals = block((own_ref, other_ref, policy_ref, extra_ref), right_refs, kernel_ref, acc, cols)
    totals = [done_ref[b] for b in range(NEAR)] + totals
    for b, total in enumerate(totals):
        at = home(place_ref, b)
        for peer in range(COLUMNS):
            sums_ref[peer, at] = total


def second_kernel(place_ref, near_ref, far_ref, parts_ref, own_ref, other_ref, *refs):
    right_refs = (own_ref.at[place_ref[2]], *refs[: COLUMNS - 1])
    image_ref, side_ref, matched = refs[COLUMNS - 1 :]
    factor = NACT / (TILE * LEFT * COLUMNS)
    for b, right_ref in enumerate(right_refs):
        at = home(place_ref, b)
        total = parts_ref[0, at]
        for peer in range(1, COLUMNS):
            total += parts_ref[peer, at]
        total = total * factor
        if b == 0:
            side_ref[...] = total
        low = total.astype(bf16).astype(f32)
        chosen = right_ref[FEAT_AT : FEAT_AT + NACT, :].astype(f32)
        made = jnp.concatenate([chosen[c : c + 1] * low for c in range(NACT)], axis=0)
        matched[:, b * TILE : (b + 1) * TILE] = made.astype(bf16)
    core = place_ref[0]
    cut = NEAR * TILE
    for step in range(PLANES // CHUNK):
        whole = slice(step * SPAN, (step + 1) * SPAN)
        out = jnp.dot(matched[:, :cut], near_ref[:, whole], preferred_element_type=f32)
        out += jnp.dot(matched[:, cut:], far_ref[:, whole], preferred_element_type=f32)
        for j in range(step * CHUNK, (step + 1) * CHUNK):
            for half, ref in enumerate((own_ref, other_ref)):
                chosen = ref[j, FEAT_AT : FEAT_AT + NACT, :].astype(f32)
                at = (2 * (j - step * CHUNK) + half) * TILE
                total = jnp.zeros((NPOL, TILE), f32)
                for c in range(NACT):
                    total += out[c * NPOL : (c + 1) * NPOL, at : at + TILE] * chosen[c : c + 1]
                image_ref[2 * j + jnp.where(core == half, 0, 1)] = total * factor


def third_kernel(parts_ref, side_ref, rewards_ref, image_ref, sums_ref):
    total = parts_ref[0]
    for i in range(1, LEFT):
        total += parts_ref[i]
    side = side_ref[...]
    image = total + ridge * side
    image_ref[...] = image
    lane = lax.broadcasted_iota(i32, (NPOL, TILE), 1)
    row = lax.broadcasted_iota(i32, (NPOL, TILE), 0)
    spread = jnp.zeros((NPOL, TILE), f32)
    for k, value in enumerate((side * side, side * image, rewards_ref[...] * side)):
        spread = jnp.where(lane == row + k * NPOL, jnp.sum(value, axis=1, keepdims=True), spread)
    flat = jnp.sum(spread, axis=0, keepdims=True)
    sums_ref[...] = jnp.broadcast_to(flat, sums_ref.shape)


def last_kernel(sums_ref, image_ref, side_ref, weights_ref, residual_ref, values_ref):
    count = sums_ref.shape[0]
    total = jnp.sum(sums_ref[...], axis=0, keepdims=True)
    lane = lax.broadcasted_iota(i32, (NPOL, TILE), 1)
    row = lax.broadcasted_iota(i32, (NPOL, TILE), 0)
    wide = jnp.broadcast_to(total, (NPOL, TILE))

    def pick(k):
        return jnp.sum(jnp.where(lane == row + k * NPOL, wide, 0.0), axis=1, keepdims=True)

    alpha = pick(0) / pick(1)
    side = side_ref[...]
    weights_ref[...] = alpha * side
    residual_ref[...] = side - alpha * image_ref[...]
    values = alpha * pick(2) / (TILE * count)
    values_ref[...] = jnp.sum(jnp.where(lane == row, values, 0.0), axis=0, keepdims=True)[:, :NPOL]


def params(limit=32 * MIB):
    return pltpu.CompilerParams(vmem_limit_bytes=limit)


def exchange(value, axes):
    return lax.all_to_all(value, axes, 0, 0)


def on_device(contexts, logged_actions, policy_actions, rewards):
    core = lax.axis_index("core")
    column = lax.axis_index(COLUMN)
    place = jnp.stack([core, column, lax.axis_index(PLANE)]).astype(i32)
    sds = jax.ShapeDtypeStruct
    vmem = pl.BlockSpec(memory_space=pltpu.VMEM)
    smem = pl.BlockSpec(memory_space=pltpu.SMEM)

    plane_send, mine = pl.pallas_call(
        prepare,
        in_specs=[pl.BlockSpec(memory_space=pl.ANY)] * 3,
        out_shape=(sds((PLANES, ROWS, D), bf16), sds((RIGHT_ROWS, D), bf16)),
        scratch_shapes=[
            pltpu.VMEM((TILE, D), bf16),
            pltpu.VMEM((1, TILE), i32),
            pltpu.VMEM((NPOL, TILE), i32),
            pltpu.SemaphoreType.DMA((3,)),
        ],
        compiler_params=params(60 * MIB),
    )(contexts, logged_actions.reshape(1, TILE), policy_actions.T)
    ring = lambda shift: [(i, (i + shift) % COLUMNS) for i in range(COLUMNS)]
    right = [lax.ppermute(mine, COLUMN, ring(shift)) for shift in range(1, COLUMNS)]
    own, *right[:BESIDE] = lax.optimization_barrier((exchange(plane_send, PLANE), *right[:BESIDE]))
    other = lax.ppermute(own, "core", [(0, 1), (1, 0)])

    policy, extra = pl.pallas_call(
        policy_kernel,
        out_shape=(sds((TILE, LEFT * TILE), bf16), sds((LEFT, TILE, TILE), bf16)),
        cost_estimate=pl.CostEstimate(flops=60_000_000, bytes_accessed=3_000_000, transcendentals=0),
        compiler_params=params(),
    )(own, other)
    left = (place, own, other, policy, extra)
    rows = LEFT * TILE

    def cost(width):
        return pl.CostEstimate(
            flops=2 * rows * width * (2 * D + TILE), bytes_accessed=2 * rows * (width + 4 * D), transcendentals=rows * width
        )

    near, far = NEAR * TILE, (COLUMNS - NEAR) * TILE
    scratch = lambda width: [pltpu.VMEM((TILE, width), f32), pltpu.VMEM((width, 2 * D), bf16)]
    near_block, done = pl.pallas_call(
        first_half,
        in_specs=[smem] + [vmem] * (3 + NEAR),
        out_shape=(sds((near, rows), bf16), sds((NEAR, NPOL, TILE), f32)),
        scratch_shapes=scratch(near),
        cost_estimate=cost(near),
        compiler_params=params(),
    )(*left, *right[: NEAR - 1])
    far_block, first = pl.pallas_call(
        second_half,
        in_specs=[smem] + [vmem] * (5 + COLUMNS - NEAR),
        out_shape=(sds((far, rows), bf16), sds((COLUMNS, COLUMNS, NPOL, TILE), f32)),
        scratch_shapes=scratch(far),
        cost_estimate=cost(far),
        compiler_params=params(),
    )(*left, done, *right[NEAR - 1 :])
    parts = exchange(first, COLUMN)
    image_parts, side = pl.pallas_call(
        second_kernel,
        in_specs=[smem] + [vmem] * (4 + COLUMNS),
        out_shape=(sds((LEFT, NPOL, TILE), f32), sds((NPOL, TILE), f32)),
        scratch_shapes=[pltpu.VMEM((TILE, COLUMNS * TILE), bf16)],
        compiler_params=params(),
    )(place, near_block, far_block, parts, own, other, *right)
    image_parts = exchange(image_parts, PLANE + ("core",))

    count = LEFT * COLUMNS
    image, sums = pl.pallas_call(
        third_kernel,
                out_shape=(sds((NPOL, TILE), f32), sds((count, TILE), f32)),
        compiler_params=params(),
    )(image_parts, side, rewards.reshape(1, TILE))
    sums = exchange(sums.reshape(count, 1, TILE), EVERY).reshape(count, TILE)
    weights, residual, values = pl.pallas_call(
        last_kernel,
        out_shape=(sds((NPOL, TILE), f32), sds((NPOL, TILE), f32), sds((1, NPOL), f32)),
        compiler_params=params(),
    )(sums, image, side)
    return weights.T, residual.T, values.reshape(NPOL)


def solution(mesh):
    fine = Mesh(mesh.devices.reshape([size for _, size in SIZES]), EVERY)
    return jax.shard_map(
        on_device,
        mesh=fine,
        in_specs=(P(EVERY, None), P(EVERY), P(EVERY, None), P(EVERY)),
        out_specs=(P(EVERY, None), P(EVERY, None), P()),
        check_vma=False,
    )
```

```python
import math

import jax
import jax.numpy as jnp
from jax import lax
from jax.experimental import pallas as pl
from jax.experimental.pallas import tpu as pltpu
from jax.sharding import Mesh
from jax.sharding import PartitionSpec as P

NPOL = 8
NACT = 16
CATALOG = 131042
D = 128
TILE = 128

ridge = 0.1
stride_base = 1009
phase_step = 0.37
two_pi = 2.0 * math.pi

SIZES = (("z_hi", 2), ("x", 4), ("z_lo", 4), ("y", 4), ("core", 2))
EVERY = tuple(name for name, _ in SIZES)
PLANE = ("x", "y")
COLUMN = ("z_hi", "z_lo")
PLANES = 16
COLUMNS = 8
LEFT = 2 * PLANES
ROWS = 160
FEAT_AT, CODE_AT = 128, 144
RIGHT_ROWS = 144

f32, bf16, i32 = jnp.float32, jnp.bfloat16, jnp.int32
MIB = 1 << 20


def wrap(product):
    guess = (product.astype(f32) * (1.0 / CATALOG)).astype(i32)
    left = product - guess * CATALOG
    left = jnp.where(left < 0, left + CATALOG, left)
    return jnp.where(left >= CATALOG, left - CATALOG, left)


def cos_sin(turn):
    eighth = (turn.astype(f32) * (4.0 / CATALOG) + 0.5).astype(i32)
    rest = 4 * turn - eighth * CATALOG
    t = rest.astype(f32) * (two_pi / 4 / CATALOG)
    u = t * t
    s = t * (1.0 + u * (-1.0 / 6 + u * (1.0 / 120 + u * (-1.0 / 5040 + u * (1.0 / 362880)))))
    c = 1.0 + u * (-0.5 + u * (1.0 / 24 + u * (-1.0 / 720 + u * (1.0 / 40320))))
    swap = (eighth == 1) | (eighth == 3)
    a = jnp.where(swap, s, c)
    b = jnp.where(swap, c, s)
    a = jnp.where((eighth == 1) | (eighth == 2), -a, a)
    b = jnp.where((eighth == 2) | (eighth == 3), -b, b)
    return a, b


def features(chosen):
    amp = math.sqrt(2.0 / NACT)
    c0, s0 = cos_sin(chosen)
    cz, sz = cos_sin(wrap(chosen * stride_base))
    pc, ps = math.cos(phase_step), math.sin(phase_step)
    zr = cz * pc - sz * ps
    zi = cz * ps + sz * pc
    wr, wi = c0 * amp, s0 * amp
    out = [jnp.full(chosen.shape, 1.0 / math.sqrt(NACT), f32)]
    for _ in range(1, NACT):
        wr, wi = wr * zr - wi * zi, wr * zi + wi * zr
        out.append(wr)
    return out


def prepare(ctx_hbm, logged_hbm, policy_hbm, plane_hbm, mine_hbm, ctx_ref, small_ref, logged_ref, policy_ref, sems, outs):
    moves = [
        pltpu.make_async_copy(source, target, sems.at[i])
        for i, (source, target) in enumerate(
            ((ctx_hbm, ctx_ref), (logged_hbm, logged_ref), (policy_hbm, policy_ref))
        )
    ]
    for move in moves:
        move.start()
    for move in moves[1:]:
        move.wait()
    logged = jnp.concatenate(features(logged_ref[...]), axis=0)
    acts = policy_ref[...]
    codes = jnp.concatenate([acts >> 9, (acts & 511) - 256], axis=0).astype(f32)
    small_ref[...] = jnp.concatenate([logged, codes], axis=0).astype(bf16)
    moves[0].wait()
    pairs = [(ctx_ref, plane_hbm.at[i, :TILE]) for i in range(PLANES)]
    pairs += [(small_ref, plane_hbm.at[i, TILE:]) for i in range(PLANES)]
    pairs += [(ctx_ref, mine_hbm.at[:TILE]), (small_ref.at[:NACT], mine_hbm.at[TILE:])]
    sends = [pltpu.make_async_copy(source, target, outs.at[i]) for i, (source, target) in enumerate(pairs)]
    for send in sends:
        send.start()
    for send in sends:
        send.wait()


def pieces(total):
    high = total.astype(bf16).astype(f32)
    rest = total - high
    middle = rest.astype(bf16).astype(f32)
    return high, middle, rest - middle


def lanes():
    return lax.broadcasted_iota(i32, (TILE, TILE), 1)


def policy_kernel(own_ref, other_ref, policy_ref, extra_ref):
    lane = lanes()
    for half, ref in enumerate((own_ref, other_ref)):
        for j in range(PLANES):
            at = 2 * j + half
            codes = ref[j, CODE_AT:ROWS, :].astype(f32).astype(i32)
            acts = (codes[:NPOL] << 9) + codes[NPOL:] + 256
            feats = jnp.concatenate(features(acts), axis=0).astype(bf16)
            policy_ref[:, at * TILE : (at + 1) * TILE] = feats
            wide = ref[j, :TILE, :].astype(f32)
            high, middle, low = pieces(jnp.sum(wide * wide, axis=1, keepdims=True))
            extra = jnp.where(lane == 0, high, jnp.where(lane == 1, middle, jnp.where(lane == 2, low, 1.0)))
            extra_ref[at] = extra.astype(bf16)


SCALE = math.log2(math.e) / D
CHUNK = 4
NEAR = 4
BESIDE = 4
SPAN = 2 * CHUNK * TILE


def home(place_ref, shift):
    return lax.rem(place_ref[1] + (COLUMNS - shift), COLUMNS)


def block(left_refs, right_refs, kernel_ref, acc, cols):
    own_ref, other_ref, policy_ref, extra_ref = left_refs
    lane = lanes()
    for b, right_ref in enumerate(right_refs):
        here = slice(b * TILE, (b + 1) * TILE)
        x = right_ref[:TILE, :].astype(f32)
        high, middle, low = pieces(jnp.sum(x * x, axis=1, keepdims=True))
        extra = jnp.where(lane < 3, -1.0, 0.0)
        for at, piece in ((3, high), (4, middle), (5, low)):
            extra = jnp.where(lane == at, -piece, extra)
        cols[here, :D] = (2.0 * x).astype(bf16)
        cols[here, D:] = extra.astype(bf16)
    for step in range(PLANES // CHUNK):
        for j in range(step * CHUNK, (step + 1) * CHUNK):
            rows = jnp.concatenate(
                [
                    jnp.concatenate([ref[j, :TILE, :], extra_ref[2 * j + half]], axis=1)
                    for half, ref in enumerate((own_ref, other_ref))
                ],
                axis=0,
            )
            expo = lax.dot_general(cols[...], rows, (((1,), (1,)), ((), ())), preferred_element_type=f32)
            kernel_ref[:, 2 * j * TILE : 2 * (j + 1) * TILE] = jnp.exp2(SCALE * expo).astype(bf16)
        whole = slice(step * SPAN, (step + 1) * SPAN)
        term = lax.dot_general(
            policy_ref[:, whole], kernel_ref[:, whole], (((1,), (1,)), ((), ())), preferred_element_type=f32
        )
        if step:
            term += acc[...]
        acc[...] = term
    sums = []
    for b, right_ref in enumerate(right_refs):
        chosen = right_ref[FEAT_AT : FEAT_AT + NACT, :].astype(f32)
        total = jnp.zeros((NPOL, TILE), f32)
        for c in range(NACT):
            total += acc[c * NPOL : (c + 1) * NPOL, b * TILE : (b + 1) * TILE] * chosen[c : c + 1]
        sums.append(total)
    return sums


def first_half(place_ref, own_ref, other_ref, policy_ref, extra_ref, *refs):
    right_refs = (own_ref.at[place_ref[2]], *refs[: NEAR - 1])
    kernel_ref, sums_ref, acc, cols = refs[NEAR - 1 :]
    for b, total in enumerate(block((own_ref, other_ref, policy_ref, extra_ref), right_refs, kernel_ref, acc, cols)):
        sums_ref[b] = total


def second_half(place_ref, own_ref, other_ref, policy_ref, extra_ref, done_ref, *refs):
    right_refs = refs[: COLUMNS - NEAR]
    kernel_ref, sums_ref, acc, cols = refs[COLUMNS - NEAR :]
    totals = block((own_ref, other_ref, policy_ref, extra_ref), right_refs, kernel_ref, acc, cols)
    totals = [done_ref[b] for b in range(NEAR)] + totals
    for b, total in enumerate(totals):
        at = home(place_ref, b)
        for peer in range(COLUMNS):
            sums_ref[peer, at] = total


def second_kernel(place_ref, near_ref, far_ref, parts_ref, own_ref, other_ref, *refs):
    right_refs = (own_ref.at[place_ref[2]], *refs[: COLUMNS - 1])
    image_ref, side_ref, matched = refs[COLUMNS - 1 :]
    factor = NACT / (TILE * LEFT * COLUMNS)
    for b, right_ref in enumerate(right_refs):
        at = home(place_ref, b)
        total = parts_ref[0, at]
        for peer in range(1, COLUMNS):
            total += parts_ref[peer, at]
        total = total * factor
        if b == 0:
            side_ref[...] = total
        low = total.astype(bf16).astype(f32)
        chosen = right_ref[FEAT_AT : FEAT_AT + NACT, :].astype(f32)
        made = jnp.concatenate([chosen[c : c + 1] * low for c in range(NACT)], axis=0)
        matched[:, b * TILE : (b + 1) * TILE] = made.astype(bf16)
    core = place_ref[0]
    cut = NEAR * TILE
    for step in range(PLANES // CHUNK):
        whole = slice(step * SPAN, (step + 1) * SPAN)
        out = jnp.dot(matched[:, :cut], near_ref[:, whole], preferred_element_type=f32)
        out += jnp.dot(matched[:, cut:], far_ref[:, whole], preferred_element_type=f32)
        for j in range(step * CHUNK, (step + 1) * CHUNK):
            for half, ref in enumerate((own_ref, other_ref)):
                chosen = ref[j, FEAT_AT : FEAT_AT + NACT, :].astype(f32)
                at = (2 * (j - step * CHUNK) + half) * TILE
                total = jnp.zeros((NPOL, TILE), f32)
                for c in range(NACT):
                    total += out[c * NPOL : (c + 1) * NPOL, at : at + TILE] * chosen[c : c + 1]
                image_ref[2 * j + jnp.where(core == half, 0, 1)] = total * factor


def third_kernel(parts_ref, side_ref, rewards_ref, image_ref, sums_ref):
    total = parts_ref[0]
    for i in range(1, LEFT):
        total += parts_ref[i]
    side = side_ref[...]
    image = total + ridge * side
    image_ref[...] = image
    lane = lax.broadcasted_iota(i32, (NPOL, TILE), 1)
    row = lax.broadcasted_iota(i32, (NPOL, TILE), 0)
    spread = jnp.zeros((NPOL, TILE), f32)
    for k, value in enumerate((side * side, side * image, rewards_ref[...] * side)):
        spread = jnp.where(lane == row + k * NPOL, jnp.sum(value, axis=1, keepdims=True), spread)
    flat = jnp.sum(spread, axis=0, keepdims=True)
    sums_ref[...] = jnp.broadcast_to(flat, sums_ref.shape)


def last_kernel(sums_ref, image_ref, side_ref, weights_ref, residual_ref, values_ref):
    count = sums_ref.shape[0]
    total = jnp.sum(sums_ref[...], axis=0, keepdims=True)
    lane = lax.broadcasted_iota(i32, (NPOL, TILE), 1)
    row = lax.broadcasted_iota(i32, (NPOL, TILE), 0)
    wide = jnp.broadcast_to(total, (NPOL, TILE))

    def pick(k):
        return jnp.sum(jnp.where(lane == row + k * NPOL, wide, 0.0), axis=1, keepdims=True)

    alpha = pick(0) / pick(1)
    side = side_ref[...]
    weights_ref[...] = alpha * side
    residual_ref[...] = side - alpha * image_ref[...]
    values = alpha * pick(2) / (TILE * count)
    values_ref[...] = jnp.sum(jnp.where(lane == row, values, 0.0), axis=0, keepdims=True)[:, :NPOL]


def params(limit=32 * MIB):
    return pltpu.CompilerParams(vmem_limit_bytes=limit)


def exchange(value, axes):
    return lax.all_to_all(value, axes, 0, 0)


def on_device(contexts, logged_actions, policy_actions, rewards):
    core = lax.axis_index("core")
    column = lax.axis_index(COLUMN)
    place = jnp.stack([core, column, lax.axis_index(PLANE)]).astype(i32)
    sds = jax.ShapeDtypeStruct
    vmem = pl.BlockSpec(memory_space=pltpu.VMEM)
    smem = pl.BlockSpec(memory_space=pltpu.SMEM)

    plane_send, mine = pl.pallas_call(
        prepare,
        in_specs=[pl.BlockSpec(memory_space=pl.ANY)] * 3,
        out_specs=(pl.BlockSpec(memory_space=pl.ANY),) * 2,
        out_shape=(sds((PLANES, ROWS, D), bf16), sds((RIGHT_ROWS, D), bf16)),
        scratch_shapes=[
            pltpu.VMEM((TILE, D), bf16),
            pltpu.VMEM((ROWS - TILE, D), bf16),
            pltpu.VMEM((1, TILE), i32),
            pltpu.VMEM((NPOL, TILE), i32),
            pltpu.SemaphoreType.DMA((3,)),
            pltpu.SemaphoreType.DMA((2 * PLANES + 2,)),
        ],
        compiler_params=params(60 * MIB),
    )(contexts, logged_actions.reshape(1, TILE), policy_actions.T)
    ring = lambda shift: [(i, (i + shift) % COLUMNS) for i in range(COLUMNS)]
    right = [lax.ppermute(mine, COLUMN, ring(shift)) for shift in range(1, COLUMNS)]
    own, *right[:BESIDE] = lax.optimization_barrier((exchange(plane_send, PLANE), *right[:BESIDE]))
    other = lax.ppermute(own, "core", [(0, 1), (1, 0)])

    policy, extra = pl.pallas_call(
        policy_kernel,
        out_shape=(sds((TILE, LEFT * TILE), bf16), sds((LEFT, TILE, TILE), bf16)),
        cost_estimate=pl.CostEstimate(flops=60_000_000, bytes_accessed=3_000_000, transcendentals=0),
        compiler_params=params(),
    )(own, other)
    left = (place, own, other, policy, extra)
    rows = LEFT * TILE

    def cost(width):
        return pl.CostEstimate(
            flops=2 * rows * width * (2 * D + TILE), bytes_accessed=2 * rows * (width + 4 * D), transcendentals=rows * width
        )

    near, far = NEAR * TILE, (COLUMNS - NEAR) * TILE
    scratch = lambda width: [pltpu.VMEM((TILE, width), f32), pltpu.VMEM((width, 2 * D), bf16)]
    near_block, done = pl.pallas_call(
        first_half,
        in_specs=[smem] + [vmem] * (3 + NEAR),
        out_shape=(sds((near, rows), bf16), sds((NEAR, NPOL, TILE), f32)),
        scratch_shapes=scratch(near),
        cost_estimate=cost(near),
        compiler_params=params(),
    )(*left, *right[: NEAR - 1])
    far_block, first = pl.pallas_call(
        second_half,
        in_specs=[smem] + [vmem] * (5 + COLUMNS - NEAR),
        out_shape=(sds((far, rows), bf16), sds((COLUMNS, COLUMNS, NPOL, TILE), f32)),
        scratch_shapes=scratch(far),
        cost_estimate=cost(far),
        compiler_params=params(),
    )(*left, done, *right[NEAR - 1 :])
    parts = exchange(first, COLUMN)
    image_parts, side = pl.pallas_call(
        second_kernel,
        in_specs=[smem] + [vmem] * (4 + COLUMNS),
        out_shape=(sds((LEFT, NPOL, TILE), f32), sds((NPOL, TILE), f32)),
        scratch_shapes=[pltpu.VMEM((TILE, COLUMNS * TILE), bf16)],
        compiler_params=params(),
    )(place, near_block, far_block, parts, own, other, *right)
    image_parts = exchange(image_parts, PLANE + ("core",))

    count = LEFT * COLUMNS
    image, sums = pl.pallas_call(
        third_kernel,
                out_shape=(sds((NPOL, TILE), f32), sds((count, TILE), f32)),
        compiler_params=params(),
    )(image_parts, side, rewards.reshape(1, TILE))
    sums = exchange(sums.reshape(count, 1, TILE), EVERY).reshape(count, TILE)
    weights, residual, values = pl.pallas_call(
        last_kernel,
        out_shape=(sds((NPOL, TILE), f32), sds((NPOL, TILE), f32), sds((1, NPOL), f32)),
        compiler_params=params(),
    )(sums, image, side)
    return weights.T, residual.T, values.reshape(NPOL)


def solution(mesh):
    fine = Mesh(mesh.devices.reshape([size for _, size in SIZES]), EVERY)
    return jax.shard_map(
        on_device,
        mesh=fine,
        in_specs=(P(EVERY, None), P(EVERY), P(EVERY, None), P(EVERY)),
        out_specs=(P(EVERY, None), P(EVERY, None), P()),
        check_vma=False,
    )
```
